32 devices in a mesh: grp: 2 (over x), seq: 8 (over z, y), tp: 2 (over core).
Axes of the slice: x: 2, y: 2, z: 4, core: 2. Of those that a mesh axis runs over, the one named last changes fastest.
Arguments:
- x_in: bfloat16 [4096, 8192], P(('grp', 'seq'), 'tp'), parts along dimension 0, may hold values from -6 to 6
- z_in: bfloat16 [4096, 8192], P(('grp', 'seq'), 'tp'), parts along dimension 0, may hold values from -6 to 6
- bc_in: bfloat16 [2, 4096, 1024], P(None, ('grp', 'seq'), 'tp'), parts along dimension 1, may hold values from -6 to 6
- dt_raw: float32 [4096, 128], P(('grp', 'seq'), 'tp'), parts along dimension 0, may hold values from -4 to 24
- conv_x: bfloat16 [4, 8192], P(None, 'tp'), may hold values from -3 to 3
- conv_bc: bfloat16 [2, 4, 1024], P(None, None, 'tp'), may hold values from -3 to 3
- a_log: float32 [128], P('tp'), may hold values from -6 to 4
- dt_bias: float32 [128], P('tp'), may hold values from -7.4 to -6.4
- d_skip: float32 [128], P('tp'), may hold values from 0.5 to 2
- gain: float32 [8192], P('tp'), may hold values from 0.1 to 1.9
- sign_bits: int32 [8192], P('tp'), may hold values from 0 to 1
- out_weight: bfloat16 [8192, 2048], P('tp', 'seq'), may hold values from -0.0625 to 0.0625
Outputs:
- out: bfloat16 [4096, 2048], P(('grp', 'seq'), 'tp'), parts along dimension 0
The draws below stay inside these ranges and needn't reach their ends.
There are 2 independent parts, one for each index of `grp`. The reference program is written for one: setup_inputs(seed, part) draws one part's arguments, and reference() takes and returns one part's arrays. A program takes and returns all parts, laid end to end along the dimension named above; an argument that names none is the same for every part. Nothing has to cross between parts.
All inputs are finite; a program needn't handle non-finite values.
Results may differ from the reference program's by a relative error of at most 0.013.
Values may be sent and summed in bfloat16 or wider, within the bound.
No kernel may reach another device: no remote copies, remote signals or barrier semaphores. Data moves between devices by JAX's collectives and lax.ppermute only.
A program may use at most 320 MiB of HBM per device.

```python
import jax
import jax.numpy as jnp
from jax import lax

HEADS = 128
HEADDIM = 64
STATE = 128
GROUPS = 8
KERNEL = 4
BLOCK = 256
OUT_WIDTH = 2048
INNER = 8192
LENGTH = 2048


def draw_a_log(key, part):
    key_pick, key_slow, key_fast = jax.random.split(key, 3)
    lifted_by = 3 * (128 // STATE - 1) // 7
    slow_heads = jax.random.uniform(key_pick, (HEADS,)) < 0.5
    slow_rate = jnp.log(0.3 / LENGTH) + jax.random.uniform(key_slow, (HEADS,)) * jnp.log(2.0 / 0.3)
    fast_rate = jnp.log(1.0 / 50.0) + jax.random.uniform(key_fast, (HEADS,)) * jnp.log(50.0 / 30.0)
    return (jnp.where(slow_heads, slow_rate, fast_rate) + jnp.log(1000.0) - lifted_by).astype(jnp.float32)


def draw_dt_raw(key, part):
    key_base, key_block, key_spots, key_extra = jax.random.split(key, 4)
    block_count = LENGTH // BLOCK
    lifted_by = 3 * (128 // STATE - 1) // 7
    base_noise = 0.5 * jax.random.truncated_normal(key_base, -3.0, 3.0, (LENGTH, HEADS))
    offsets = jax.random.uniform(key_block, (block_count, 1, HEADS), minval=-0.7, maxval=0.7)
    base_noise = (base_noise.reshape(block_count, BLOCK, HEADS) + offsets).reshape(LENGTH, HEADS)
    spots = jax.random.randint(key_spots, (4,), 0, LENGTH)
    bursting = jnp.any(jnp.arange(LENGTH)[:, None] == spots[None, :], axis=1)
    target = 0.00052 * LENGTH * jnp.exp(jnp.float32(lifted_by))
    lifted = jnp.log(jnp.expm1(target)) + 6.9 - lifted_by + 0.3 * jax.random.uniform(key_extra, (LENGTH, HEADS), minval=-1.0, maxval=1.0)
    return jnp.where(bursting[:, None], lifted, base_noise).astype(jnp.float32)


def set_ends(result, own_key, smallest, largest):
    longest = result.shape.index(max(result.shape))
    spots = []
    for shift in (0, 1):
        where = [jax.random.randint(jax.random.fold_in(own_key, axis), (), 0, length) for axis, length in enumerate(result.shape)]
        where[longest] = (where[longest] + shift) % result.shape[longest]
        spots.append(tuple(where))
    return result.at[spots[0]].set(smallest).at[spots[1]].set(largest)


def shard_levels(stream_key, dims, cuts, low, high):
    loudness = 1.0
    for position, shards_of in cuts:
        steps = jax.random.uniform(jax.random.fold_in(jax.random.fold_in(stream_key, 6), position), (shards_of,), jnp.float32, low / len(cuts), high / len(cuts))
        loudness = loudness * jnp.repeat(jnp.exp(steps), dims[position] // shards_of).reshape((-1,) + (1,) * (len(dims) - 1 - position))
    return loudness


def gaussian(rng, shape, scale, reach, pieces=(), held_as=jnp.bfloat16):
    entries = jax.random.normal(rng, shape, jnp.float32) * scale
    if len(pieces) > 0:
        entries = shard_levels(rng, shape, pieces, -0.22, 0.18) * entries
    return jnp.clip(entries, min=-reach, max=reach).astype(held_as)


def setup_inputs(seed: int = 0, part: int = 0) -> dict:
    arg_keys = jax.random.split(jax.random.key(seed), 13)
    part_keys = jax.random.split(jax.random.fold_in(arg_keys[12], part), 13)
    return {
        "x_in": gaussian(part_keys[0], (LENGTH, INNER), 1.0, 6.0, ((0, 8), (1, 2))),
        "z_in": gaussian(part_keys[1], (LENGTH, INNER), 1.0, 6.0, ((0, 8), (1, 2))),
        "bc_in": gaussian(part_keys[2], (2, LENGTH, GROUPS * STATE), 1.0, 6.0, ((1, 8), (2, 2))),
        "dt_raw": draw_dt_raw(jax.random.fold_in(jax.random.fold_in(arg_keys[12], part), 71), part),
        "conv_x": gaussian(arg_keys[4], (KERNEL, INNER), KERNEL ** -0.5, 3.0, ((1, 2),)),
        "conv_bc": gaussian(arg_keys[5], (2, KERNEL, GROUPS * STATE), KERNEL ** -0.5, 3.0, ((2, 2),)),
        "a_log": draw_a_log(jax.random.fold_in(arg_keys[12], 71), part),
        "dt_bias": jnp.clip(-7.4 + 1.0 * jax.random.uniform(arg_keys[7], (HEADS,), jnp.float32) ** shard_levels(arg_keys[7], (HEADS,), ((0, 2),), -0.2, 0.2), -7.4, -6.4),
        "d_skip": jnp.clip(0.5 + 1.5 * jax.random.uniform(arg_keys[8], (HEADS,), jnp.float32) ** shard_levels(arg_keys[8], (HEADS,), ((0, 2),), -0.2, 0.2), 0.5, 2.0),
        "gain": jnp.clip(1.0 + 0.18 * jax.random.normal(arg_keys[9], (INNER,), jnp.float32), 0.1, 1.9),
        "sign_bits": set_ends(jax.random.randint(arg_keys[10], (INNER,), 0, 2), jax.random.fold_in(arg_keys[10], 1), 0, 1).astype(jnp.int32),
        "out_weight": gaussian(arg_keys[11], (INNER, OUT_WIDTH), INNER ** -0.5, 0.0625, ((0, 2), (1, 8))),
    }


def conv_silu(padded, kernel_rows, length_out):
    summed = jnp.zeros(padded.shape[:-2] + (length_out, padded.shape[-1]), jnp.float32)
    for offset in range(len(kernel_rows)):
        summed = summed + padded[..., offset:offset + length_out, :].astype(jnp.float32) * kernel_rows[offset].astype(jnp.float32)
    return jax.nn.silu(summed).astype(jnp.bfloat16)

def group_terms(x_grp, b_grp, c_grp, cum_grp, dt_grp):
    scores = jnp.einsum('ktn,ksn->kts', c_grp.astype(jnp.float32), b_grp.astype(jnp.float32), precision=lax.Precision.HIGHEST)
    extent = cum_grp.shape[1]
    cum_heads = jnp.swapaxes(cum_grp, 1, 2)
    dt_heads = jnp.swapaxes(dt_grp, 1, 2)
    causal = (jnp.arange(extent)[:, None] >= jnp.arange(extent)[None, :])[None, None, :, :]
    exponent = jnp.where(causal, cum_heads[:, :, :, None] - cum_heads[:, :, None, :], 0.0)
    weights = jnp.where(causal, scores[:, None, :, :] * jnp.exp(exponent) * dt_heads[:, :, None, :], 0.0).astype(jnp.bfloat16)
    within = jnp.einsum('kjts,ksjp->ktjp', weights.astype(jnp.float32), x_grp.astype(jnp.float32), precision=lax.Precision.HIGHEST)
    to_end = jnp.exp(cum_grp[:, -1:, :] - cum_grp) * dt_grp
    loaded = (b_grp[:, :, None, :].astype(jnp.float32) * to_end[..., None]).astype(jnp.bfloat16)
    states = jnp.einsum('ksjn,ksjp->kjpn', loaded.astype(jnp.float32), x_grp.astype(jnp.float32), precision=lax.Precision.HIGHEST)
    return (within, states)

def hadamard(values):
    row_count, breadth = values.shape
    half_size = 1
    for doubling in range(breadth.bit_length() - 1):
        shaped = values.reshape(row_count, breadth // (2 * half_size), 2, half_size)
        values = jnp.concatenate([shaped[:, :, :1] + shaped[:, :, 1:], shaped[:, :, :1] - shaped[:, :, 1:]], axis=2).reshape(row_count, breadth)
        half_size = half_size * 2
    return values

def reference(x_in, z_in, bc_in, dt_raw, conv_x, conv_bc, a_log, dt_bias, d_skip, gain, sign_bits, out_weight):
    length_all = x_in.shape[0]
    kernel = conv_x.shape[0]
    x_pad = jnp.concatenate([jnp.zeros((kernel - 1, INNER), jnp.bfloat16), x_in], axis=0)
    x_conv = conv_silu(x_pad, [conv_x[offset] for offset in range(kernel)], length_all)
    bc_pad = jnp.concatenate([jnp.zeros((2, kernel - 1, GROUPS * STATE), jnp.bfloat16), bc_in], axis=1)
    bc_conv = conv_silu(bc_pad, [conv_bc[:, offset][:, None, :] for offset in range(kernel)], length_all)
    dt_step = jax.nn.softplus(dt_raw + dt_bias)
    log_decay = dt_step * -jnp.exp(a_log)
    blocks = length_all // BLOCK
    per_group = HEADS // GROUPS
    cumulative = jnp.cumsum(log_decay.reshape(blocks, BLOCK, HEADS), axis=1)
    x_blocks = x_conv.reshape(blocks, BLOCK, GROUPS, per_group, HEADDIM)
    b_blocks = bc_conv[0].reshape(blocks, BLOCK, GROUPS, STATE)
    c_blocks = bc_conv[1].reshape(blocks, BLOCK, GROUPS, STATE)
    cum_g = cumulative.reshape(blocks, BLOCK, GROUPS, per_group)
    dt_g = dt_step.reshape(blocks, BLOCK, GROUPS, per_group)
    within, states = lax.map(lambda packed: group_terms(*packed), (jnp.moveaxis(x_blocks, 2, 0), jnp.moveaxis(b_blocks, 2, 0), jnp.moveaxis(c_blocks, 2, 0), jnp.moveaxis(cum_g, 2, 0), jnp.moveaxis(dt_g, 2, 0)))
    within = jnp.moveaxis(within, 0, 2).reshape(blocks, BLOCK, HEADS, HEADDIM)
    states = jnp.moveaxis(states, 0, 1).reshape(blocks, HEADS, HEADDIM, STATE)
    end_decay = jnp.exp(cumulative[:, -1, :])

    def advance(running, element):
        decay_here, state_here = element
        return (running * decay_here[:, None, None] + state_here, running)
    start_state = jnp.zeros((HEADS, HEADDIM, STATE), jnp.float32)
    last_state, incoming = lax.scan(advance, start_state, (end_decay, states))
    carried = jnp.einsum('kcgn,kgjpn->kcgjp', c_blocks.astype(jnp.float32), incoming.reshape(blocks, GROUPS, per_group, HEADDIM, STATE), precision=lax.Precision.HIGHEST)
    carried = carried.reshape(blocks, BLOCK, HEADS, HEADDIM) * jnp.exp(cumulative)[..., None]
    skipped = d_skip[:, None] * x_conv.reshape(blocks, BLOCK, HEADS, HEADDIM).astype(jnp.float32)
    y_full = (within + carried + skipped).reshape(length_all, INNER)
    gated = y_full * jax.nn.silu(z_in.astype(jnp.float32))
    grouped = gated.reshape(length_all, GROUPS, INNER // GROUPS)
    mean_sq = lax.optimization_barrier(jnp.mean(grouped * grouped, axis=-1, keepdims=True))
    normed = ((grouped * lax.rsqrt(mean_sq + 1e-05)).reshape(length_all, INNER) * gain).astype(jnp.bfloat16)
    signed = normed * (1 - 2 * sign_bits).astype(jnp.bfloat16)
    rotated = (hadamard(signed.astype(jnp.float32)) / jnp.sqrt(jnp.float32(INNER))).astype(jnp.bfloat16)
    return jnp.dot(rotated, out_weight, preferred_element_type=jnp.float32).astype(jnp.bfloat16)
```

```python
import math

import jax
import jax.numpy as jnp
from jax import lax
from jax.experimental import pallas as pl
from jax.experimental.pallas import tpu as pltpu
from jax.sharding import Mesh
from jax.sharding import PartitionSpec as P

HEADDIM = 64
STATE = 128
BLOCK = 256
INNER = 8192
GROUP = 1024
PER = 16
AXES = ("grp", "sz", "sy", "tp")
LOG2E = 1.4426950408889634
F32 = jnp.float32
BF16 = jnp.bfloat16
HIGH = lax.Precision.HIGHEST
VM = pl.BlockSpec(memory_space=pltpu.VMEM)


def send(array, route):
    sizes = [lax.axis_size(a) for a in AXES]
    pairs = []
    for x in range(sizes[0]):
        for z in range(sizes[1]):
            for y in range(sizes[2]):
                for t in range(sizes[3]):
                    to = route(x, z, y, t)
                    if to is None or not 0 <= to[1] < sizes[1]:
                        continue
                    source = ((x * sizes[1] + z) * sizes[2] + y) * sizes[3] + t
                    target = ((to[0] * sizes[1] + to[1]) * sizes[2] + to[2]) * sizes[3] + to[3]
                    pairs.append((source, target))
    return lax.ppermute(array, AXES, pairs)


def swap(array, k):
    return send(array, lambda x, z, y, t: (x ^ (k >> 1), z, y ^ (k & 1), t))


def onward(array, distance):
    return send(array, lambda x, z, y, t: (x, z + distance, y, t))


def expander():
    row = lax.broadcasted_iota(jnp.int32, (PER, GROUP), 0)
    lane = lax.broadcasted_iota(jnp.int32, (PER, GROUP), 1)
    return jnp.where(lane // HEADDIM == row, 1.0, 0.0).astype(F32)


def silu(v):
    return v * lax.logistic(v)


def pack_kernel(order, x0, x1, x2, x3, b0, b1, b2, b3, dt, o0, o1, o2, o3, d0, d1, d2, d3, turned):
    turned[...] = dt[...].T
    for k, (x, b, o, d) in enumerate(
        ((x0, b0, o0, d0), (x1, b1, o1, d1), (x2, b2, o2, d2), (x3, b3, o3, d3))
    ):
        o[:, :GROUP] = x[...]
        o[:, GROUP : GROUP + STATE] = b[0]
        o[:, GROUP + STATE :] = b[1]
        first = pl.multiple_of(order[k] * PER, PER)
        d[...] = turned[pl.ds(first, PER), :]


def pack(order, x_in, bc_in, dt_raw):
    rows = x_in.shape[0]
    wide = GROUP + 2 * STATE
    whole = lambda *shape: pl.BlockSpec(shape, lambda i, order: (0,) * len(shape))
    return pl.pallas_call(
        pack_kernel,
        grid_spec=pltpu.PrefetchScalarGridSpec(
            num_scalar_prefetch=1,
            grid=(1,),
            in_specs=[
                pl.BlockSpec((rows, GROUP), lambda i, order, k=k: (0, order[k])) for k in range(4)
            ]
            + [
                pl.BlockSpec((2, rows, STATE), lambda i, order, k=k: (0, 0, order[k]))
                for k in range(4)
            ]
            + [whole(rows, dt_raw.shape[1])],
            out_specs=[whole(rows, wide)] * 4 + [whole(PER, rows)] * 4,
            scratch_shapes=[pltpu.VMEM((dt_raw.shape[1], rows), F32)],
        ),
        out_shape=[jax.ShapeDtypeStruct((rows, wide), BF16)] * 4
        + [jax.ShapeDtypeStruct((PER, rows), F32)] * 4,
        name="pack",
    )(order, x_in, x_in, x_in, x_in, bc_in, bc_in, bc_in, bc_in, dt_raw)


def cut_kernel(order, z1, z2, z3, o1, o2, o3):
    o1[...] = z1[...]
    o2[...] = z2[...]
    o3[...] = z3[...]


def cut(order, z_in):
    rows = z_in.shape[0]
    return pl.pallas_call(
        cut_kernel,
        grid_spec=pltpu.PrefetchScalarGridSpec(
            num_scalar_prefetch=1,
            grid=(1,),
            in_specs=[
                pl.BlockSpec((rows, GROUP), lambda i, order, k=k: (0, order[k]))
                for k in range(1, 4)
            ],
            out_specs=[pl.BlockSpec((rows, GROUP), lambda i, order: (0, 0))] * 3,
        ),
        out_shape=[jax.ShapeDtypeStruct((rows, GROUP), BF16)] * 3,
        name="cut",
    )(order, z_in, z_in, z_in)


def turn_kernel(sign, w, out, mid):
    size = 256
    chunks = w.shape[0] // size
    half = chunks // 2
    row = lax.broadcasted_iota(jnp.int32, (size, size), 0)
    col = lax.broadcasted_iota(jnp.int32, (size, size), 1)
    shared = row & col
    parity = jnp.zeros((size, size), jnp.int32)
    for position in range(8):
        parity = parity ^ ((shared >> position) & 1)
    small = (1 - 2 * parity).astype(F32).astype(BF16)
    for j in range(chunks):
        mid[j] = jnp.dot(small, w[j * size : (j + 1) * size, :], preferred_element_type=F32)
    scale = 1.0 / math.sqrt(INNER)
    upper = jnp.where(sign[0] == 0, scale, -scale)

    def step(i, carry):
        at = pl.ds(pl.multiple_of(i * 16, 16), 16)
        values = [mid[j, at, :] * scale + mid[j + half, at, :] * upper for j in range(half)]
        width = 1
        while width < half:
            fresh = list(values)
            for j in range(half):
                if j & width == 0:
                    fresh[j] = values[j] + values[j + width]
                    fresh[j + width] = values[j] - values[j + width]
            values = fresh
            width *= 2
        for j in range(half):
            out[j, at, :] = values[j].astype(BF16)
        return carry

    lax.fori_loop(0, size // 16, step, 0)


def turn(sign, weight):
    rows, cols = weight.shape
    return pl.pallas_call(
        turn_kernel,
        in_specs=[pl.BlockSpec(memory_space=pltpu.SMEM), VM],
        out_specs=VM,
        out_shape=jax.ShapeDtypeStruct((rows // 512, 256, cols), BF16),
        scratch_shapes=[pltpu.VMEM((rows // 256, 256, cols), F32)],
        name="turn",
    )(sign, weight)


def conv_kernel(
    place, p0, p1, p2, p3, halo, cx, cbc, d0, d1, d2, d3, al, db,
    xc, bc, low, cum, pair, first, fade, states, decays,
):
    here = place[1]
    pieces = (p0, p1, p2, p3)
    steps = (d0, d1, d2, d3)
    rows = p0.shape[0]
    spread = expander()
    row = lax.broadcasted_iota(jnp.int32, (rows, rows), 0)
    col = lax.broadcasted_iota(jnp.int32, (rows, rows), 1)
    upto = jnp.where(row <= col, 1.0, 0.0).astype(F32)
    for k in range(4):
        piece, other = pieces[k], pieces[k ^ 1]
        opening = here == (k & 1)

        def conv(at, taps):
            outer = halo[k >> 1, :, at].astype(F32)
            inner = other[rows - 16 :, at].astype(F32)
            before = jnp.where(opening, outer, inner)[8:]
            padded = jnp.concatenate([before, piece[:, at].astype(F32)], axis=0)
            summed = padded[5 : 5 + rows] * taps[0:1]
            for tap in range(1, 4):
                summed = summed + padded[5 + tap : 5 + tap + rows] * taps[tap : tap + 1]
            return silu(summed).astype(BF16)

        def chunk(c, carry, conv=conv, k=k):
            at = pl.ds(pl.multiple_of(c * 128, 128), 128)
            xc[k, :, at] = conv(at, cx[:, at].astype(F32))
            return carry

        lax.fori_loop(0, GROUP // 128, chunk, 0)
        b = conv(slice(GROUP, GROUP + STATE), cbc[0].astype(F32))
        c = conv(slice(GROUP + STATE, GROUP + 2 * STATE), cbc[1].astype(F32))
        bc[k, :, :STATE] = b
        bc[k, :, STATE:] = c
        raw = steps[k][...] + db[...]
        dt = jnp.maximum(raw, 0.0) + jnp.log1p(jnp.exp(-jnp.abs(raw)))
        rate = -jnp.exp(al[...])
        total = jnp.dot(dt * rate, upto, precision=HIGH, preferred_element_type=F32)
        low[k] = (total - jnp.log(dt)) * LOG2E
        upright = total.T
        cum[k] = upright
        load = (jnp.exp(total[:, rows - 1 :] - total) * dt).T
        wide = jnp.dot(load, spread, precision=HIGH, preferred_element_type=F32)
        loaded = (xc[k].astype(F32) * wide).astype(BF16)
        states[k] = lax.dot_general(
            b, loaded, (((0,), (0,)), ((), ())), preferred_element_type=F32
        )
        end = jnp.broadcast_to(jnp.exp(upright[rows - 1 :, :]), (8, PER))
        decays[k] = jnp.dot(end, spread, precision=HIGH, preferred_element_type=F32)
    for r in range(2):
        early, late = 2 * r + here, 2 * r + 1 - here
        decay_early, decay_late = decays[early], decays[late]
        pair[r, :STATE, :] = (states[late] + decay_late[0:1] * states[early]).astype(BF16)
        pair[r, STATE:, :] = split(decay_early * decay_late)
        first[r] = states[early]
        fade[r] = decay_early


def split(decay):
    high = decay.astype(BF16).astype(F32)
    middle = (decay - high).astype(BF16).astype(F32)
    last = decay - high - middle
    both = jnp.concatenate([decay, decay], axis=0)
    row = lax.broadcasted_iota(jnp.int32, both.shape, 0)
    twice = lambda v: jnp.concatenate([v, v], axis=0)
    out = jnp.where(row == 0, twice(high), jnp.where(row == 1, twice(middle), twice(last)))
    return jnp.where(row < 3, out, 0.0).astype(BF16)


def joined(tail):
    tail = tail.astype(F32)
    return tail[0:1] + tail[1:2] + tail[2:3]


def conv_states(place, pieces, halo, conv_x, conv_bc, steps, a_log, dt_bias):
    rows = pieces[0].shape[0]
    whole = lambda *shape: pl.BlockSpec(shape, lambda i, place: (0,) * len(shape))
    shapes = [
        ((4, rows, GROUP), BF16),
        ((4, rows, 2 * STATE), BF16),
        ((4, PER, rows), F32),
        ((4, rows, PER), F32),
        ((2, STATE + 16, GROUP), BF16),
        ((2, STATE, GROUP), F32),
        ((2, 8, GROUP), F32),
    ]
    return pl.pallas_call(
        conv_kernel,
        grid_spec=pltpu.PrefetchScalarGridSpec(
            num_scalar_prefetch=1,
            grid=(1,),
            in_specs=[whole(rows, GROUP + 2 * STATE)] * 4
            + [
                whole(2, 16, GROUP + 2 * STATE),
                pl.BlockSpec((4, GROUP), lambda i, place: (0, place[0])),
                pl.BlockSpec((2, 4, STATE), lambda i, place: (0, 0, place[0])),
            ]
            + [whole(PER, rows)] * 4
            + [pl.BlockSpec((PER, 1), lambda i, place: (place[0], 0))] * 2,
            out_specs=[whole(*shape) for shape, _ in shapes],
            scratch_shapes=[
                pltpu.VMEM((4, STATE, GROUP), F32),
                pltpu.VMEM((4, 8, GROUP), F32),
            ],
        ),
        out_shape=[jax.ShapeDtypeStruct(shape, kind) for shape, kind in shapes],
        name="conv_states",
    )(place, *pieces, halo, conv_x, conv_bc, *steps, a_log, dt_bias)


def join_kernel(late, early, out):
    for r in range(2):
        decay = joined(late[r, STATE:, :])
        out[r, :STATE, :] = (
            late[r, :STATE, :].astype(F32) + decay * early[r, :STATE, :].astype(F32)
        ).astype(BF16)
        both = decay * joined(early[r, STATE:, :])
        out[r, STATE:, :] = split(jnp.broadcast_to(both, (8, GROUP)))


def join(late, early):
    return pl.pallas_call(
        join_kernel,
        in_specs=[VM, VM],
        out_specs=VM,
        out_shape=jax.ShapeDtypeStruct(late.shape, BF16),
        name="join",
    )(late, early)


def within_kernel(place, xc, bc, low, cum, skip, out):
    rows = xc.shape[1]
    half = rows // 2
    b = bc[0, :, :STATE]
    c = bc[0, :, STATE:]
    scores = lax.dot_general(c, b, (((1,), (1,)), ((), ())), preferred_element_type=F32)
    row = lax.broadcasted_iota(jnp.int32, (half, half), 0)
    col = lax.broadcasted_iota(jnp.int32, (half, half), 1)
    causal = row >= col
    corner = jnp.where(causal, scores[:half, :half], 0.0)
    square = scores[half:, :half]
    end = jnp.where(causal, scores[half:, half:], 0.0)
    lane = lax.broadcasted_iota(jnp.int32, (rows, 2 * HEADDIM), 1)
    upright = cum[0] * LOG2E
    for j in range(PER // 2):
        at = slice(j * 2 * HEADDIM, (j + 1) * 2 * HEADDIM)
        x = xc[0, :, at]
        top = bottom = None
        for side in range(2):
            h = 2 * j + side
            mine = jnp.where((lane < HEADDIM) == (side == 0), x, jnp.zeros_like(x))
            level = upright[:, h : h + 1]
            floor = low[0, h : h + 1, :]
            one = jnp.exp2(jnp.minimum(level[:half] - floor[:, :half], 64.0)) * corner
            two = jnp.exp2(level[half:] - floor[:, :half]) * square
            three = jnp.exp2(jnp.minimum(level[half:] - floor[:, half:], 64.0)) * end
            low_rows = jnp.concatenate([two.astype(BF16), three.astype(BF16)], axis=1)
            first = jnp.dot(one.astype(BF16), mine[:half], preferred_element_type=F32)
            last = jnp.dot(low_rows, mine, preferred_element_type=F32)
            top = first if top is None else top + first
            bottom = last if bottom is None else bottom + last
        skipped = x.astype(F32) * skip[:, at]
        out[0, :half, at] = top + skipped[:half]
        out[0, half:, at] = bottom + skipped[half:]


def within(place, xc, bc, low, cum, skip):
    rows = xc.shape[1]
    block = lambda *shape: pl.BlockSpec((1,) + shape, lambda k, place: (k, 0, 0))
    return pl.pallas_call(
        within_kernel,
        grid_spec=pltpu.PrefetchScalarGridSpec(
            num_scalar_prefetch=1,
            grid=(4,),
            in_specs=[
                block(rows, GROUP),
                block(rows, 2 * STATE),
                block(PER, rows),
                block(rows, PER),
                pl.BlockSpec((1, GROUP), lambda k, place: (0, place[0])),
            ],
            out_specs=block(rows, GROUP),
        ),
        out_shape=jax.ShapeDtypeStruct((4, rows, GROUP), F32),
        name="within",
    )(place, xc, bc, low, cum, skip)


def gate_kernel(
    place, y, bc, cum, near, far, first, fade, z0, z1, z2, z3, gain, bits, out, gate
):
    k = pl.program_id(0)
    for index, z in enumerate((z0, z1, z2, z3)):

        @pl.when(k == index)
        def _(z=z):
            gate[...] = silu(z[...].astype(F32))

    opening = place[1] == (k % 2)
    incoming = near[0, :STATE, :].astype(F32) + joined(near[0, STATE:, :]) * far[
        0, :STATE, :
    ].astype(F32)
    incoming = jnp.where(opening, incoming, fade[0, 0:1] * incoming + first[0])
    carried = jnp.dot(bc[0, :, STATE:], incoming.astype(BF16), preferred_element_type=F32)
    kept = jnp.dot(jnp.exp(cum[0]), expander(), precision=HIGH, preferred_element_type=F32)
    gated = (y[0] + kept * carried) * gate[...]
    scale = lax.rsqrt(jnp.mean(gated * gated, axis=1, keepdims=True) + 1e-05)
    signed = gain[...] * (1 - 2 * bits[...]).astype(F32)
    out[0] = (gated * scale * signed).astype(BF16)


def gate_norm(place, y, bc, cum, near, far, first, fade, z_in, zs, gain, bits):
    rows = y.shape[1]
    block = lambda *shape: pl.BlockSpec((1,) + shape, lambda k, place: (k, 0, 0))
    part = lambda *shape: pl.BlockSpec((1,) + shape, lambda k, place: (k // 2, 0, 0))
    mine = lambda rows: pl.BlockSpec((rows, GROUP), lambda k, place: (0, place[0]))
    return pl.pallas_call(
        gate_kernel,
        grid_spec=pltpu.PrefetchScalarGridSpec(
            num_scalar_prefetch=1,
            grid=(4,),
            in_specs=[
                block(rows, GROUP),
                block(rows, 2 * STATE),
                block(rows, PER),
                part(STATE + 16, GROUP),
                part(STATE + 16, GROUP),
                part(STATE, GROUP),
                part(8, GROUP),
                mine(rows),
            ]
            + [pl.BlockSpec((rows, GROUP), lambda k, place: (0, 0))] * 3
            + [mine(1), mine(1)],
            out_specs=block(rows, GROUP),
            scratch_shapes=[pltpu.VMEM((rows, GROUP), F32)],
        ),
        out_shape=jax.ShapeDtypeStruct((4, rows, GROUP), BF16),
        name="gate_norm",
    )(place, y, bc, cum, near, far, first, fade, z_in, *zs, gain, bits)


def per_device(
    x_in, z_in, bc_in, dt_raw, conv_x, conv_bc, a_log, dt_bias, d_skip, gain, sign_bits, out_weight
):
    rows = x_in.shape[0]
    x_here, y_here, t_here = (lax.axis_index(a) for a in ("grp", "sy", "tp"))
    length = lax.axis_size("sz")
    mine = 2 * x_here + y_here
    order = jnp.stack([mine ^ k for k in range(4)]).astype(jnp.int32)
    place = jnp.stack([mine, y_here]).astype(jnp.int32)

    packed = pack(order, x_in, bc_in, dt_raw)
    pieces = [packed[0]] + [swap(packed[k], k) for k in range(1, 4)]
    steps = [packed[4]] + [swap(packed[4 + k], k) for k in range(1, 4)]
    tails = [p[rows - 16 :] for p in pieces]
    closing = jnp.where(
        y_here == 1, jnp.stack([tails[0], tails[2]]), jnp.stack([tails[1], tails[3]])
    )
    halo = onward(closing, 1)

    turned = turn(x_here.reshape(1).astype(jnp.int32), out_weight)
    turned = turned.reshape(2, GROUP, out_weight.shape[1])
    across = send(turned, lambda x, z, y, t: (x, z, y, 1 - t))
    own = turned.astype(F32)
    rotated = (across.astype(F32) + jnp.where(t_here == 0, own, -own)).astype(BF16)
    kept = lax.dynamic_index_in_dim(rotated, y_here, 0, keepdims=False)
    given = swap(lax.dynamic_index_in_dim(rotated, 1 - y_here, 0, keepdims=False), 1)
    columns = jnp.where(
        y_here == 0,
        jnp.concatenate([kept, given], axis=1),
        jnp.concatenate([given, kept], axis=1),
    )
    weight = lax.all_gather(columns, "sz", axis=1, tiled=True)

    zs = [swap(z, k + 1) for k, z in enumerate(cut(order, z_in))]

    xc, bc, low, cum, pair, first, fade = conv_states(
        place, pieces, halo, conv_x, conv_bc, steps, a_log[:, None], dt_bias[:, None]
    )
    near = onward(pair, 1)
    y = within(place, xc, bc, low, cum, jnp.repeat(d_skip, HEADDIM)[None])
    span = join(pair, near)
    distance = 2
    far = onward(span, distance)
    while 2 * distance < length:
        near, span = join(near, far), join(span, far)
        distance *= 2
        far = onward(span, distance)
    act = gate_norm(
        place, y, bc, cum, near, far, first, fade, z_in, zs, gain[None], sign_bits[None]
    )

    act = act.reshape(4 * rows, GROUP)
    half = weight.shape[1] // 2
    theirs = lax.dynamic_slice_in_dim(weight, (1 - t_here) * half, half, 1)
    ours = lax.dynamic_slice_in_dim(weight, t_here * half, half, 1)
    away = jnp.dot(act, theirs, preferred_element_type=F32).astype(BF16)
    back = send(away, lambda x, z, y, t: (x, z, y, 1 - t))
    stay = jnp.dot(act, ours, preferred_element_type=F32) + back.astype(F32)
    stay = stay.reshape(4, rows, half)
    total = stay[0]
    for k in range(1, 4):
        total = total + swap(stay[k].astype(BF16), k).astype(F32)
    return total.astype(BF16)


def solution(mesh):
    shape = mesh.devices.shape
    fine = Mesh(mesh.devices.reshape(shape[0], shape[1] // 2, 2, shape[2]), AXES)
    seq = ("sz", "sy")
    rows = ("grp",) + seq
    in_specs = (
        P(rows, "tp"),
        P(rows, "tp"),
        P(None, rows, "tp"),
        P(rows, "tp"),
        P(None, "tp"),
        P(None, None, "tp"),
        P("tp"),
        P("tp"),
        P("tp"),
        P("tp"),
        P("tp"),
        P("tp", seq),
    )
    return jax.shard_map(
        per_device, mesh=fine, in_specs=in_specs, out_specs=P(rows, "tp"), check_vma=False
    )
```

```python
import math

import jax
import jax.numpy as jnp
from jax import lax
from jax.experimental import pallas as pl
from jax.experimental.pallas import tpu as pltpu
from jax.sharding import Mesh
from jax.sharding import PartitionSpec as P

HEADDIM = 64
STATE = 128
BLOCK = 256
INNER = 8192
GROUP = 1024
PER = 16
AXES = ("grp", "sz", "sy", "tp")
LOG2E = 1.4426950408889634
F32 = jnp.float32
BF16 = jnp.bfloat16
HIGH = lax.Precision.HIGHEST
VM = pl.BlockSpec(memory_space=pltpu.VMEM)


def send(array, route):
    sizes = [lax.axis_size(a) for a in AXES]
    pairs = []
    for x in range(sizes[0]):
        for z in range(sizes[1]):
            for y in range(sizes[2]):
                for t in range(sizes[3]):
                    to = route(x, z, y, t)
                    if to is None or not 0 <= to[1] < sizes[1]:
                        continue
                    source = ((x * sizes[1] + z) * sizes[2] + y) * sizes[3] + t
                    target = ((to[0] * sizes[1] + to[1]) * sizes[2] + to[2]) * sizes[3] + to[3]
                    pairs.append((source, target))
    return lax.ppermute(array, AXES, pairs)


def swap(array, k):
    return send(array, lambda x, z, y, t: (x ^ (k >> 1), z, y ^ (k & 1), t))


def onward(array, distance):
    return send(array, lambda x, z, y, t: (x, z + distance, y, t))


def after(these, those):
    return lax.optimization_barrier((these, those))


def expander():
    row = lax.broadcasted_iota(jnp.int32, (3 * PER, GROUP), 0)
    lane = lax.broadcasted_iota(jnp.int32, (3 * PER, GROUP), 1)
    return jnp.where(lane // HEADDIM == row % PER, 1.0, 0.0).astype(BF16)


def thirds(v):
    high = v.astype(BF16)
    rest = v - high.astype(F32)
    middle = rest.astype(BF16)
    last = (rest - middle.astype(F32)).astype(BF16)
    return jnp.concatenate([high, middle, last], axis=0)


def widen(terms, spread):
    return lax.dot_general(terms, spread, (((0,), (0,)), ((), ())), preferred_element_type=F32)


def silu(v):
    half = 0.5 * v
    return half + half * jnp.tanh(half)


def pack_kernel(order, x0, x1, x2, x3, b0, b1, b2, b3, dt, o0, o1, o2, o3, d0, d1, d2, d3, turned):
    turned[...] = dt[...].T
    for k, (x, b, o, d) in enumerate(
        ((x0, b0, o0, d0), (x1, b1, o1, d1), (x2, b2, o2, d2), (x3, b3, o3, d3))
    ):
        o[:, :GROUP] = x[...]
        o[:, GROUP : GROUP + STATE] = b[0]
        o[:, GROUP + STATE :] = b[1]
        first = pl.multiple_of(order[k] * PER, PER)
        d[...] = turned[pl.ds(first, PER), :]


def pack(order, x_in, bc_in, dt_raw):
    rows = x_in.shape[0]
    wide = GROUP + 2 * STATE
    whole = lambda *shape: pl.BlockSpec(shape, lambda i, order: (0,) * len(shape))
    return pl.pallas_call(
        pack_kernel,
        grid_spec=pltpu.PrefetchScalarGridSpec(
            num_scalar_prefetch=1,
            grid=(1,),
            in_specs=[
                pl.BlockSpec((rows, GROUP), lambda i, order, k=k: (0, order[k])) for k in range(4)
            ]
            + [
                pl.BlockSpec((2, rows, STATE), lambda i, order, k=k: (0, 0, order[k]))
                for k in range(4)
            ]
            + [whole(rows, dt_raw.shape[1])],
            out_specs=[whole(rows, wide)] * 4 + [whole(PER, rows)] * 4,
            scratch_shapes=[pltpu.VMEM((dt_raw.shape[1], rows), F32)],
        ),
        out_shape=[jax.ShapeDtypeStruct((rows, wide), BF16)] * 4
        + [jax.ShapeDtypeStruct((PER, rows), F32)] * 4,
        name="pack",
    )(order, x_in, x_in, x_in, x_in, bc_in, bc_in, bc_in, bc_in, dt_raw)


def cut_kernel(order, z1, z2, z3, o1, o2, o3):
    o1[...] = z1[...]
    o2[...] = z2[...]
    o3[...] = z3[...]


def cut(order, z_in):
    rows = z_in.shape[0]
    return pl.pallas_call(
        cut_kernel,
        grid_spec=pltpu.PrefetchScalarGridSpec(
            num_scalar_prefetch=1,
            grid=(1,),
            in_specs=[
                pl.BlockSpec((rows, GROUP), lambda i, order, k=k: (0, order[k]))
                for k in range(1, 4)
            ],
            out_specs=[pl.BlockSpec((rows, GROUP), lambda i, order: (0, 0))] * 3,
        ),
        out_shape=[jax.ShapeDtypeStruct((rows, GROUP), BF16)] * 3,
        name="cut",
    )(order, z_in, z_in, z_in)


def turn_kernel(sign, w, out, mid):
    size = 256
    chunks = w.shape[0] // size
    half = chunks // 2
    row = lax.broadcasted_iota(jnp.int32, (size, size), 0)
    col = lax.broadcasted_iota(jnp.int32, (size, size), 1)
    shared = row & col
    parity = jnp.zeros((size, size), jnp.int32)
    for position in range(8):
        parity = parity ^ ((shared >> position) & 1)
    small = (1 - 2 * parity).astype(F32).astype(BF16)
    for j in range(chunks):
        mid[j] = jnp.dot(small, w[j * size : (j + 1) * size, :], preferred_element_type=F32)
    scale = 1.0 / math.sqrt(INNER)
    upper = jnp.where(sign[0] == 0, scale, -scale)

    def step(i, carry):
        at = pl.ds(pl.multiple_of(i * 16, 16), 16)
        values = [mid[j, at, :] * scale + mid[j + half, at, :] * upper for j in range(half)]
        width = 1
        while width < half:
            fresh = list(values)
            for j in range(half):
                if j & width == 0:
                    fresh[j] = values[j] + values[j + width]
                    fresh[j + width] = values[j] - values[j + width]
            values = fresh
            width *= 2
        for j in range(half):
            out[j, at, :] = values[j].astype(BF16)
        return carry

    lax.fori_loop(0, size // 16, step, 0)


def turn(sign, weight):
    rows, cols = weight.shape
    return pl.pallas_call(
        turn_kernel,
        in_specs=[pl.BlockSpec(memory_space=pltpu.SMEM), VM],
        out_specs=VM,
        out_shape=jax.ShapeDtypeStruct((rows // 512, 256, cols), BF16),
        scratch_shapes=[pltpu.VMEM((rows // 256, 256, cols), F32)],
        name="turn",
    )(sign, weight)


def conv_kernel(
    place, p0, p1, p2, p3, halo, cx, cbc, d0, d1, d2, d3, al, db,
    xc, bc, low, cum, kept, pair, first, fade, states, decays,
):
    here = place[1]
    pieces = (p0, p1, p2, p3)
    steps = (d0, d1, d2, d3)
    rows = p0.shape[0]
    spread = expander()
    row = lax.broadcasted_iota(jnp.int32, (rows, rows), 0)
    col = lax.broadcasted_iota(jnp.int32, (rows, rows), 1)
    upto = jnp.where(row <= col, 1.0, 0.0).astype(BF16)
    for k in range(4):
        piece, other = pieces[k], pieces[k ^ 1]
        opening = here == (k & 1)

        def conv(at, taps):
            outer = halo[k >> 1, :, at].astype(F32)
            inner = other[rows - 16 :, at].astype(F32)
            before = jnp.where(opening, outer, inner)[8:]
            padded = jnp.concatenate([before, piece[:, at].astype(F32)], axis=0)
            summed = padded[5 : 5 + rows] * taps[0:1]
            for tap in range(1, 4):
                summed = summed + padded[5 + tap : 5 + tap + rows] * taps[tap : tap + 1]
            return silu(summed).astype(BF16)

        def chunk(c, carry, conv=conv, k=k):
            at = pl.ds(pl.multiple_of(c * 128, 128), 128)
            xc[k, :, at] = conv(at, cx[:, at].astype(F32))
            return carry

        lax.fori_loop(0, GROUP // 128, chunk, 0)
        b = conv(slice(GROUP, GROUP + STATE), cbc[0].astype(F32))
        c = conv(slice(GROUP + STATE, GROUP + 2 * STATE), cbc[1].astype(F32))
        bc[k, :, :STATE] = b
        bc[k, :, STATE:] = c
        raw = steps[k][...] + db[...]
        dt = jnp.maximum(raw, 0.0) + jnp.log1p(jnp.exp(-jnp.abs(raw)))
        rate = -jnp.exp(al[...])
        sums = jnp.dot(thirds(dt * rate), upto, preferred_element_type=F32)
        total = sums[:PER] + sums[PER : 2 * PER] + sums[2 * PER :]
        low[k] = (total - jnp.log(dt)) * LOG2E
        cum[k] = (total * LOG2E).T
        fall = jnp.exp(total)
        kept[k] = thirds(fall)
        wide = widen(thirds(jnp.exp(total[:, rows - 1 :] - total) * dt), spread)
        loaded = (xc[k].astype(F32) * wide).astype(BF16)
        states[k] = lax.dot_general(
            b, loaded, (((0,), (0,)), ((), ())), preferred_element_type=F32
        )
        decays[k] = widen(kept[k, :, rows - 128 :], spread)[120:]
    for r in range(2):
        early, late = 2 * r + here, 2 * r + 1 - here
        decay_early, decay_late = decays[early], decays[late]
        pair[r, :STATE, :] = (states[late] + decay_late[7:8] * states[early]).astype(BF16)
        pair[r, STATE:, :] = split(jnp.broadcast_to((decay_early * decay_late)[7:8], (8, GROUP)))
        first[r] = states[early]
        fade[r] = decay_early


def split(decay):
    high = decay.astype(BF16).astype(F32)
    middle = (decay - high).astype(BF16).astype(F32)
    last = decay - high - middle
    both = jnp.concatenate([decay, decay], axis=0)
    row = lax.broadcasted_iota(jnp.int32, both.shape, 0)
    twice = lambda v: jnp.concatenate([v, v], axis=0)
    out = jnp.where(row == 0, twice(high), jnp.where(row == 1, twice(middle), twice(last)))
    return jnp.where(row < 3, out, 0.0).astype(BF16)


def joined(tail):
    tail = tail.astype(F32)
    return tail[0:1] + tail[1:2] + tail[2:3]


def conv_states(place, pieces, halo, conv_x, conv_bc, steps, a_log, dt_bias):
    rows = pieces[0].shape[0]
    whole = lambda *shape: pl.BlockSpec(shape, lambda i, place: (0,) * len(shape))
    shapes = [
        ((4, rows, GROUP), BF16),
        ((4, rows, 2 * STATE), BF16),
        ((4, PER, rows), F32),
        ((4, rows, PER), F32),
        ((4, 3 * PER, rows), BF16),
        ((2, STATE + 16, GROUP), BF16),
        ((2, STATE, GROUP), F32),
        ((2, 8, GROUP), F32),
    ]
    return pl.pallas_call(
        conv_kernel,
        grid_spec=pltpu.PrefetchScalarGridSpec(
            num_scalar_prefetch=1,
            grid=(1,),
            in_specs=[whole(rows, GROUP + 2 * STATE)] * 4
            + [
                whole(2, 16, GROUP + 2 * STATE),
                pl.BlockSpec((4, GROUP), lambda i, place: (0, place[0])),
                pl.BlockSpec((2, 4, STATE), lambda i, place: (0, 0, place[0])),
            ]
            + [whole(PER, rows)] * 4
            + [pl.BlockSpec((PER, 1), lambda i, place: (place[0], 0))] * 2,
            out_specs=[whole(*shape) for shape, _ in shapes],
            scratch_shapes=[
                pltpu.VMEM((4, STATE, GROUP), F32),
                pltpu.VMEM((4, 8, GROUP), F32),
            ],
        ),
        out_shape=[jax.ShapeDtypeStruct(shape, kind) for shape, kind in shapes],
        name="conv_states",
    )(place, *pieces, halo, conv_x, conv_bc, *steps, a_log, dt_bias)


def join_kernel(late, early, out):
    for r in range(2):
        decay = joined(late[r, STATE:, :])
        out[r, :STATE, :] = (
            late[r, :STATE, :].astype(F32) + decay * early[r, :STATE, :].astype(F32)
        ).astype(BF16)
        both = decay * joined(early[r, STATE:, :])
        out[r, STATE:, :] = split(jnp.broadcast_to(both, (8, GROUP)))


def join(late, early):
    return pl.pallas_call(
        join_kernel,
        in_specs=[VM, VM],
        out_specs=VM,
        out_shape=jax.ShapeDtypeStruct(late.shape, BF16),
        name="join",
    )(late, early)


def within_kernel(place, xc, bc, low, cum, skip, out):
    rows = xc.shape[1]
    half = rows // 2
    b = bc[0, :, :STATE]
    c = bc[0, :, STATE:]
    scores = lax.dot_general(c, b, (((1,), (1,)), ((), ())), preferred_element_type=F32)
    row = lax.broadcasted_iota(jnp.int32, (half, half), 0)
    col = lax.broadcasted_iota(jnp.int32, (half, half), 1)
    causal = row >= col
    corner = jnp.where(causal, scores[:half, :half], 0.0)
    square = scores[half:, :half]
    end = jnp.where(causal, scores[half:, half:], 0.0)
    lane = lax.broadcasted_iota(jnp.int32, (rows, 2 * HEADDIM), 1)
    upright = cum[0]
    for j in range(PER // 2):
        at = slice(j * 2 * HEADDIM, (j + 1) * 2 * HEADDIM)
        x = xc[0, :, at]
        top = bottom = None
        for side in range(2):
            h = 2 * j + side
            mine = jnp.where((lane < HEADDIM) == (side == 0), x, jnp.zeros_like(x))
            level = upright[:, h : h + 1]
            floor = low[0, h : h + 1, :]
            one = jnp.exp2(jnp.minimum(level[:half] - floor[:, :half], 64.0)) * corner
            two = jnp.exp2(level[half:] - floor[:, :half]) * square
            three = jnp.exp2(jnp.minimum(level[half:] - floor[:, half:], 64.0)) * end
            low_rows = jnp.concatenate([two.astype(BF16), three.astype(BF16)], axis=1)
            first = jnp.dot(one.astype(BF16), mine[:half], preferred_element_type=F32)
            last = jnp.dot(low_rows, mine, preferred_element_type=F32)
            top = first if top is None else top + first
            bottom = last if bottom is None else bottom + last
        skipped = x.astype(F32) * skip[:, at]
        out[0, :half, at] = top + skipped[:half]
        out[0, half:, at] = bottom + skipped[half:]


def within(place, xc, bc, low, cum, skip):
    rows = xc.shape[1]
    block = lambda *shape: pl.BlockSpec((1,) + shape, lambda k, place: (k, 0, 0))
    return pl.pallas_call(
        within_kernel,
        grid_spec=pltpu.PrefetchScalarGridSpec(
            num_scalar_prefetch=1,
            grid=(4,),
            in_specs=[
                block(rows, GROUP),
                block(rows, 2 * STATE),
                block(PER, rows),
                block(rows, PER),
                pl.BlockSpec((1, GROUP), lambda k, place: (0, place[0])),
            ],
            out_specs=block(rows, GROUP),
        ),
        out_shape=jax.ShapeDtypeStruct((4, rows, GROUP), F32),
        name="within",
    )(place, xc, bc, low, cum, skip)


def gate_kernel(
    place, y, bc, kept, near, far, first, fade, z0, z1, z2, z3, gain, bits, out, gate
):
    k = pl.program_id(0)
    for index, z in enumerate((z0, z1, z2, z3)):

        @pl.when(k == index)
        def _(z=z):
            gate[...] = silu(z[...].astype(F32))

    opening = place[1] == (k % 2)
    incoming = near[0, :STATE, :].astype(F32) + joined(near[0, STATE:, :]) * far[
        0, :STATE, :
    ].astype(F32)
    incoming = jnp.where(opening, incoming, fade[0, 7:8] * incoming + first[0])
    carried = jnp.dot(bc[0, :, STATE:], incoming.astype(BF16), preferred_element_type=F32)
    gated = (y[0] + widen(kept[0], expander()) * carried) * gate[...]
    scale = lax.rsqrt(jnp.mean(gated * gated, axis=1, keepdims=True) + 1e-05)
    signed = gain[...] * (1 - 2 * bits[...]).astype(F32)
    out[0] = (gated * scale * signed).astype(BF16)


def gate_norm(place, y, bc, kept, near, far, first, fade, z_in, zs, gain, bits):
    rows = y.shape[1]
    block = lambda *shape: pl.BlockSpec((1,) + shape, lambda k, place: (k, 0, 0))
    part = lambda *shape: pl.BlockSpec((1,) + shape, lambda k, place: (k // 2, 0, 0))
    mine = lambda rows: pl.BlockSpec((rows, GROUP), lambda k, place: (0, place[0]))
    return pl.pallas_call(
        gate_kernel,
        grid_spec=pltpu.PrefetchScalarGridSpec(
            num_scalar_prefetch=1,
            grid=(4,),
            in_specs=[
                block(rows, GROUP),
                block(rows, 2 * STATE),
                block(3 * PER, rows),
                part(STATE + 16, GROUP),
                part(STATE + 16, GROUP),
                part(STATE, GROUP),
                part(8, GROUP),
                mine(rows),
            ]
            + [pl.BlockSpec((rows, GROUP), lambda k, place: (0, 0))] * 3
            + [mine(1), mine(1)],
            out_specs=block(rows, GROUP),
            scratch_shapes=[pltpu.VMEM((rows, GROUP), F32)],
        ),
        out_shape=jax.ShapeDtypeStruct((4, rows, GROUP), BF16),
        name="gate_norm",
    )(place, y, bc, kept, near, far, first, fade, z_in, *zs, gain, bits)


def per_device(
    x_in, z_in, bc_in, dt_raw, conv_x, conv_bc, a_log, dt_bias, d_skip, gain, sign_bits, out_weight
):
    rows = x_in.shape[0]
    x_here, y_here, t_here = (lax.axis_index(a) for a in ("grp", "sy", "tp"))
    length = lax.axis_size("sz")
    mine = 2 * x_here + y_here
    order = jnp.stack([mine ^ k for k in range(4)]).astype(jnp.int32)
    place = jnp.stack([mine, y_here]).astype(jnp.int32)

    turned = turn(x_here.reshape(1).astype(jnp.int32), out_weight)
    turned = turned.reshape(2, GROUP, out_weight.shape[1])
    across = send(turned, lambda x, z, y, t: (x, z, y, 1 - t))

    x_in, turned = after(x_in, turned)
    packed = pack(order, x_in, bc_in, dt_raw)
    packed, across = after(packed, across)
    own = turned.astype(F32)
    rotated = (across.astype(F32) + jnp.where(t_here == 0, own, -own)).astype(BF16)
    packed, rotated = after(packed, rotated)
    keep = lax.dynamic_index_in_dim(rotated, y_here, 0, keepdims=False)
    given = swap(lax.dynamic_index_in_dim(rotated, 1 - y_here, 0, keepdims=False), 1)
    pieces = [packed[0]] + [swap(packed[k], k) for k in range(1, 4)]
    steps = [packed[4]] + [swap(packed[4 + k], k) for k in range(1, 4)]
    z_in, packed = after(z_in, packed)
    slices = cut(order, z_in)
    given, slices = after(given, slices)
    columns = jnp.where(
        y_here == 0,
        jnp.concatenate([keep, given], axis=1),
        jnp.concatenate([given, keep], axis=1),
    )
    weight = lax.all_gather(columns, "sz", axis=1, tiled=True)
    pieces, columns = after(pieces, columns)
    tails = [p[rows - 16 :] for p in pieces]
    closing = jnp.where(
        y_here == 1, jnp.stack([tails[0], tails[2]]), jnp.stack([tails[1], tails[3]])
    )
    halo = onward(closing, 1)
    slices, pieces = after(slices, pieces)
    zs = [swap(z, k + 1) for k, z in enumerate(slices)]

    xc, bc, low, cum, kept, pair, first, fade = conv_states(
        place, pieces, halo, conv_x, conv_bc, steps, a_log[:, None], dt_bias[:, None]
    )
    near = onward(pair, 1)
    y = within(place, xc, bc, low, cum, jnp.repeat(d_skip, HEADDIM)[None])
    near, y = after(near, y)
    span = join(pair, near)
    distance = 2
    far = onward(span, distance)
    while 2 * distance < length:
        near, span = join(near, far), join(span, far)
        distance *= 2
        far = onward(span, distance)
    act = gate_norm(
        place, y, bc, kept, near, far, first, fade, z_in, zs, gain[None], sign_bits[None]
    )

    act = act.reshape(4 * rows, GROUP)
    half = weight.shape[1] // 2
    theirs = lax.dynamic_slice_in_dim(weight, (1 - t_here) * half, half, 1)
    ours = lax.dynamic_slice_in_dim(weight, t_here * half, half, 1)
    away = jnp.dot(act, theirs, preferred_element_type=F32).astype(BF16)
    back = send(away, lambda x, z, y, t: (x, z, y, 1 - t))
    stay = jnp.dot(act, ours, preferred_element_type=F32) + back.astype(F32)
    stay = stay.reshape(4, rows, half)
    total = stay[0]
    for k in range(1, 4):
        total = total + swap(stay[k].astype(BF16), k).astype(F32)
    return total.astype(BF16)


def solution(mesh):
    shape = mesh.devices.shape
    fine = Mesh(mesh.devices.reshape(shape[0], shape[1] // 2, 2, shape[2]), AXES)
    seq = ("sz", "sy")
    rows = ("grp",) + seq
    in_specs = (
        P(rows, "tp"),
        P(rows, "tp"),
        P(None, rows, "tp"),
        P(rows, "tp"),
        P(None, "tp"),
        P(None, None, "tp"),
        P("tp"),
        P("tp"),
        P("tp"),
        P("tp"),
        P("tp"),
        P("tp", seq),
    )
    return jax.shard_map(
        per_device, mesh=fine, in_specs=in_specs, out_specs=P(rows, "tp"), check_vma=False
    )
```

```python
import math

import jax
import jax.numpy as jnp
from jax import lax
from jax.experimental import pallas as pl
from jax.experimental.pallas import tpu as pltpu
from jax.sharding import Mesh
from jax.sharding import PartitionSpec as P

HEADDIM = 64
STATE = 128
BLOCK = 256
INNER = 8192
GROUP = 1024
PER = 16
AXES = ("grp", "sz", "sy", "tp")
LOG2E = 1.4426950408889634
F32 = jnp.float32
BF16 = jnp.bfloat16
HIGH = lax.Precision.HIGHEST
VM = pl.BlockSpec(memory_space=pltpu.VMEM)


def send(array, route):
    sizes = [lax.axis_size(a) for a in AXES]
    pairs = []
    for x in range(sizes[0]):
        for z in range(sizes[1]):
            for y in range(sizes[2]):
                for t in range(sizes[3]):
                    to = route(x, z, y, t)
                    if to is None or not 0 <= to[1] < sizes[1]:
                        continue
                    source = ((x * sizes[1] + z) * sizes[2] + y) * sizes[3] + t
                    target = ((to[0] * sizes[1] + to[1]) * sizes[2] + to[2]) * sizes[3] + to[3]
                    pairs.append((source, target))
    return lax.ppermute(array, AXES, pairs)


def swap(array, k):
    return send(array, lambda x, z, y, t: (x ^ (k >> 1), z, y ^ (k & 1), t))


def onward(array, distance):
    return send(array, lambda x, z, y, t: (x, z + distance, y, t))


def after(these, those):
    return lax.optimization_barrier((these, those))


def expander():
    row = lax.broadcasted_iota(jnp.int32, (3 * PER, GROUP), 0)
    lane = lax.broadcasted_iota(jnp.int32, (3 * PER, GROUP), 1)
    return jnp.where(lane // HEADDIM == row % PER, 1.0, 0.0).astype(BF16)


def thirds(v):
    high = v.astype(BF16)
    rest = v - high.astype(F32)
    middle = rest.astype(BF16)
    last = (rest - middle.astype(F32)).astype(BF16)
    return jnp.concatenate([high, middle, last], axis=0)


def widen(terms, spread):
    return lax.dot_general(terms, spread, (((0,), (0,)), ((), ())), preferred_element_type=F32)


def silu(v):
    half = 0.5 * v
    return half + half * jnp.tanh(half)


def pack_kernel(order, x0, x1, x2, x3, b0, b1, b2, b3, dt, o0, o1, o2, o3, d0, d1, d2, d3, turned):
    turned[...] = dt[...].T
    for k, (x, b, o, d) in enumerate(
        ((x0, b0, o0, d0), (x1, b1, o1, d1), (x2, b2, o2, d2), (x3, b3, o3, d3))
    ):
        o[:, :GROUP] = x[...]
        o[:, GROUP : GROUP + STATE] = b[0]
        o[:, GROUP + STATE :] = b[1]
        first = pl.multiple_of(order[k] * PER, PER)
        d[...] = turned[pl.ds(first, PER), :]


def pack(order, x_in, bc_in, dt_raw):
    rows = x_in.shape[0]
    wide = GROUP + 2 * STATE
    whole = lambda *shape: pl.BlockSpec(shape, lambda i, order: (0,) * len(shape))
    return pl.pallas_call(
        pack_kernel,
        grid_spec=pltpu.PrefetchScalarGridSpec(
            num_scalar_prefetch=1,
            grid=(1,),
            in_specs=[
                pl.BlockSpec((rows, GROUP), lambda i, order, k=k: (0, order[k])) for k in range(4)
            ]
            + [
                pl.BlockSpec((2, rows, STATE), lambda i, order, k=k: (0, 0, order[k]))
                for k in range(4)
            ]
            + [whole(rows, dt_raw.shape[1])],
            out_specs=[whole(rows, wide)] * 4 + [whole(PER, rows)] * 4,
            scratch_shapes=[pltpu.VMEM((dt_raw.shape[1], rows), F32)],
        ),
        out_shape=[jax.ShapeDtypeStruct((rows, wide), BF16)] * 4
        + [jax.ShapeDtypeStruct((PER, rows), F32)] * 4,
        name="pack",
    )(order, x_in, x_in, x_in, x_in, bc_in, bc_in, bc_in, bc_in, dt_raw)


def cut_kernel(order, z1, z2, z3, o1, o2, o3):
    o1[...] = z1[...]
    o2[...] = z2[...]
    o3[...] = z3[...]


def cut(order, z_in):
    rows = z_in.shape[0]
    return pl.pallas_call(
        cut_kernel,
        grid_spec=pltpu.PrefetchScalarGridSpec(
            num_scalar_prefetch=1,
            grid=(1,),
            in_specs=[
                pl.BlockSpec((rows, GROUP), lambda i, order, k=k: (0, order[k]))
                for k in range(1, 4)
            ],
            out_specs=[pl.BlockSpec((rows, GROUP), lambda i, order: (0, 0))] * 3,
        ),
        out_shape=[jax.ShapeDtypeStruct((rows, GROUP), BF16)] * 3,
        name="cut",
    )(order, z_in, z_in, z_in)


def turn_kernel(sign, w, out, mid):
    size = 256
    chunks = w.shape[0] // size
    half = chunks // 2
    row = lax.broadcasted_iota(jnp.int32, (size, size), 0)
    col = lax.broadcasted_iota(jnp.int32, (size, size), 1)
    shared = row & col
    parity = jnp.zeros((size, size), jnp.int32)
    for position in range(8):
        parity = parity ^ ((shared >> position) & 1)
    small = (1 - 2 * parity).astype(F32).astype(BF16)
    for j in range(chunks):
        mid[j] = jnp.dot(small, w[j * size : (j + 1) * size, :], preferred_element_type=F32)
    scale = 1.0 / math.sqrt(INNER)
    upper = jnp.where(sign[0] == 0, scale, -scale)

    def step(i, carry):
        at = pl.ds(pl.multiple_of(i * 16, 16), 16)
        values = [mid[j, at, :] * scale + mid[j + half, at, :] * upper for j in range(half)]
        width = 1
        while width < half:
            fresh = list(values)
            for j in range(half):
                if j & width == 0:
                    fresh[j] = values[j] + values[j + width]
                    fresh[j + width] = values[j] - values[j + width]
            values = fresh
            width *= 2
        for j in range(half):
            out[j, at, :] = values[j].astype(BF16)
        return carry

    lax.fori_loop(0, size // 16, step, 0)


def turn(sign, weight):
    rows, cols = weight.shape
    return pl.pallas_call(
        turn_kernel,
        in_specs=[pl.BlockSpec(memory_space=pltpu.SMEM), VM],
        out_specs=VM,
        out_shape=jax.ShapeDtypeStruct((rows // 512, 256, cols), BF16),
        scratch_shapes=[pltpu.VMEM((rows // 256, 256, cols), F32)],
        name="turn",
    )(sign, weight)


def conv_kernel(
    place, p0, p1, p2, p3, halo, cx, cbc, d0, d1, d2, d3, al, db,
    xc, bc, low, cum, kept, pair, first, fade, states, decays,
):
    here = place[1]
    pieces = (p0, p1, p2, p3)
    steps = (d0, d1, d2, d3)
    rows = p0.shape[0]
    spread = expander()
    row = lax.broadcasted_iota(jnp.int32, (rows, rows), 0)
    col = lax.broadcasted_iota(jnp.int32, (rows, rows), 1)
    upto = jnp.where(row <= col, 1.0, 0.0).astype(BF16)
    for k in range(4):
        piece, other = pieces[k], pieces[k ^ 1]
        opening = here == (k & 1)

        def conv(at, taps):
            outer = halo[k >> 1, :, at].astype(F32)
            inner = other[rows - 16 :, at].astype(F32)
            before = jnp.where(opening, outer, inner)[8:]
            padded = jnp.concatenate([before, piece[:, at].astype(F32)], axis=0)
            summed = padded[5 : 5 + rows] * taps[0:1]
            for tap in range(1, 4):
                summed = summed + padded[5 + tap : 5 + tap + rows] * taps[tap : tap + 1]
            return silu(summed).astype(BF16)

        def chunk(c, carry, conv=conv, k=k):
            at = pl.ds(pl.multiple_of(c * 128, 128), 128)
            xc[k, :, at] = conv(at, cx[:, at].astype(F32))
            return carry

        lax.fori_loop(0, GROUP // 128, chunk, 0)
        b = conv(slice(GROUP, GROUP + STATE), cbc[0].astype(F32))
        c = conv(slice(GROUP + STATE, GROUP + 2 * STATE), cbc[1].astype(F32))
        bc[k, :, :STATE] = b
        bc[k, :, STATE:] = c
        raw = steps[k][...] + db[...]
        dt = jnp.maximum(raw, 0.0) + jnp.log1p(jnp.exp(-jnp.abs(raw)))
        rate = -jnp.exp(al[...])
        sums = jnp.dot(thirds(dt * rate), upto, preferred_element_type=F32)
        total = sums[:PER] + sums[PER : 2 * PER] + sums[2 * PER :]
        low[k] = (total - jnp.log(dt)) * LOG2E
        cum[k] = (total * LOG2E).T
        fall = jnp.exp(total)
        kept[k] = thirds(fall)
        wide = widen(thirds(jnp.exp(total[:, rows - 1 :] - total) * dt), spread)
        loaded = (xc[k].astype(F32) * wide).astype(BF16)
        states[k] = lax.dot_general(
            b, loaded, (((0,), (0,)), ((), ())), preferred_element_type=F32
        )
        decays[k] = widen(kept[k, :, rows - 128 :], spread)[120:]
    for r in range(2):
        early, late = 2 * r + here, 2 * r + 1 - here
        decay_early, decay_late = decays[early], decays[late]
        pair[r, :STATE, :] = (states[late] + decay_late[7:8] * states[early]).astype(BF16)
        pair[r, STATE:, :] = split(jnp.broadcast_to((decay_early * decay_late)[7:8], (8, GROUP)))
        first[r] = states[early]
        fade[r] = decay_early


def split(decay):
    high = decay.astype(BF16).astype(F32)
    middle = (decay - high).astype(BF16).astype(F32)
    last = decay - high - middle
    both = jnp.concatenate([decay, decay], axis=0)
    row = lax.broadcasted_iota(jnp.int32, both.shape, 0)
    twice = lambda v: jnp.concatenate([v, v], axis=0)
    out = jnp.where(row == 0, twice(high), jnp.where(row == 1, twice(middle), twice(last)))
    return jnp.where(row < 3, out, 0.0).astype(BF16)


def joined(tail):
    tail = tail.astype(F32)
    return tail[0:1] + tail[1:2] + tail[2:3]


def conv_states(place, pieces, halo, conv_x, conv_bc, steps, a_log, dt_bias):
    rows = pieces[0].shape[0]
    whole = lambda *shape: pl.BlockSpec(shape, lambda i, place: (0,) * len(shape))
    shapes = [
        ((4, rows, GROUP), BF16),
        ((4, rows, 2 * STATE), BF16),
        ((4, PER, rows), F32),
        ((4, rows, PER), F32),
        ((4, 3 * PER, rows), BF16),
        ((2, STATE + 16, GROUP), BF16),
        ((2, STATE, GROUP), F32),
        ((2, 8, GROUP), F32),
    ]
    return pl.pallas_call(
        conv_kernel,
        grid_spec=pltpu.PrefetchScalarGridSpec(
            num_scalar_prefetch=1,
            grid=(1,),
            in_specs=[whole(rows, GROUP + 2 * STATE)] * 4
            + [
                whole(2, 16, GROUP + 2 * STATE),
                pl.BlockSpec((4, GROUP), lambda i, place: (0, place[0])),
                pl.BlockSpec((2, 4, STATE), lambda i, place: (0, 0, place[0])),
            ]
            + [whole(PER, rows)] * 4
            + [pl.BlockSpec((PER, 1), lambda i, place: (place[0], 0))] * 2,
            out_specs=[whole(*shape) for shape, _ in shapes],
            scratch_shapes=[
                pltpu.VMEM((4, STATE, GROUP), F32),
                pltpu.VMEM((4, 8, GROUP), F32),
            ],
        ),
        out_shape=[jax.ShapeDtypeStruct(shape, kind) for shape, kind in shapes],
        name="conv_states",
    )(place, *pieces, halo, conv_x, conv_bc, *steps, a_log, dt_bias)


def join_kernel(late, early, out):
    for r in range(2):
        decay = joined(late[r, STATE:, :])
        out[r, :STATE, :] = (
            late[r, :STATE, :].astype(F32) + decay * early[r, :STATE, :].astype(F32)
        ).astype(BF16)
        both = decay * joined(early[r, STATE:, :])
        out[r, STATE:, :] = split(jnp.broadcast_to(both, (8, GROUP)))


def join(late, early):
    return pl.pallas_call(
        join_kernel,
        in_specs=[VM, VM],
        out_specs=VM,
        out_shape=jax.ShapeDtypeStruct(late.shape, BF16),
        name="join",
    )(late, early)


def within_kernel(place, xc, bc, low, cum, skip, out):
    rows = xc.shape[1]
    half = rows // 2
    b = bc[0, :, :STATE]
    c = bc[0, :, STATE:]
    scores = lax.dot_general(c, b, (((1,), (1,)), ((), ())), preferred_element_type=F32)
    row = lax.broadcasted_iota(jnp.int32, (half, half), 0)
    col = lax.broadcasted_iota(jnp.int32, (half, half), 1)
    causal = row >= col
    corner = jnp.where(causal, scores[:half, :half], 0.0)
    square = scores[half:, :half]
    end = jnp.where(causal, scores[half:, half:], 0.0)
    lane = lax.broadcasted_iota(jnp.int32, (rows, 2 * HEADDIM), 1)
    upright = cum[0]
    for j in range(PER // 2):
        at = slice(j * 2 * HEADDIM, (j + 1) * 2 * HEADDIM)
        x = xc[0, :, at]
        top = bottom = None
        for side in range(2):
            h = 2 * j + side
            mine = jnp.where((lane < HEADDIM) == (side == 0), x, jnp.zeros_like(x))
            level = upright[:, h : h + 1]
            floor = low[0, h : h + 1, :]
            one = jnp.exp2(jnp.minimum(level[:half] - floor[:, :half], 64.0)) * corner
            two = jnp.exp2(level[half:] - floor[:, :half]) * square
            three = jnp.exp2(jnp.minimum(level[half:] - floor[:, half:], 64.0)) * end
            low_rows = jnp.concatenate([two.astype(BF16), three.astype(BF16)], axis=1)
            first = jnp.dot(one.astype(BF16), mine[:half], preferred_element_type=F32)
            last = jnp.dot(low_rows, mine, preferred_element_type=F32)
            top = first if top is None else top + first
            bottom = last if bottom is None else bottom + last
        skipped = x.astype(F32) * skip[:, at]
        out[0, :half, at] = top + skipped[:half]
        out[0, half:, at] = bottom + skipped[half:]


def within(place, xc, bc, low, cum, skip):
    rows = xc.shape[1]
    block = lambda *shape: pl.BlockSpec((1,) + shape, lambda k, place: (k, 0, 0))
    return pl.pallas_call(
        within_kernel,
        grid_spec=pltpu.PrefetchScalarGridSpec(
            num_scalar_prefetch=1,
            grid=(4,),
            in_specs=[
                block(rows, GROUP),
                block(rows, 2 * STATE),
                block(PER, rows),
                block(rows, PER),
                pl.BlockSpec((1, GROUP), lambda k, place: (0, place[0])),
            ],
            out_specs=block(rows, GROUP),
        ),
        out_shape=jax.ShapeDtypeStruct((4, rows, GROUP), F32),
        name="within",
    )(place, xc, bc, low, cum, skip)


def gate_kernel(
    place, y, bc, kept, near, far, first, fade, z0, z1, z2, z3, gain, bits, out, gate
):
    k = pl.program_id(0)
    for index, z in enumerate((z0, z1, z2, z3)):

        @pl.when(k == index)
        def _(z=z):
            gate[...] = silu(z[...].astype(F32))

    opening = place[1] == (k % 2)
    incoming = near[0, :STATE, :].astype(F32) + joined(near[0, STATE:, :]) * far[
        0, :STATE, :
    ].astype(F32)
    incoming = jnp.where(opening, incoming, fade[0, 7:8] * incoming + first[0])
    carried = jnp.dot(bc[0, :, STATE:], incoming.astype(BF16), preferred_element_type=F32)
    gated = (y[0] + widen(kept[0], expander()) * carried) * gate[...]
    scale = lax.rsqrt(jnp.mean(gated * gated, axis=1, keepdims=True) + 1e-05)
    signed = gain[...] * (1 - 2 * bits[...]).astype(F32)
    out[0] = (gated * scale * signed).astype(BF16)


def gate_norm(place, y, bc, kept, near, far, first, fade, z_in, zs, gain, bits):
    rows = y.shape[1]
    block = lambda *shape: pl.BlockSpec((1,) + shape, lambda k, place: (k, 0, 0))
    part = lambda *shape: pl.BlockSpec((1,) + shape, lambda k, place: (k // 2, 0, 0))
    mine = lambda rows: pl.BlockSpec((rows, GROUP), lambda k, place: (0, place[0]))
    return pl.pallas_call(
        gate_kernel,
        grid_spec=pltpu.PrefetchScalarGridSpec(
            num_scalar_prefetch=1,
            grid=(4,),
            in_specs=[
                block(rows, GROUP),
                block(rows, 2 * STATE),
                block(3 * PER, rows),
                part(STATE + 16, GROUP),
                part(STATE + 16, GROUP),
                part(STATE, GROUP),
                part(8, GROUP),
                mine(rows),
            ]
            + [pl.BlockSpec((rows, GROUP), lambda k, place: (0, 0))] * 3
            + [mine(1), mine(1)],
            out_specs=block(rows, GROUP),
            scratch_shapes=[pltpu.VMEM((rows, GROUP), F32)],
        ),
        out_shape=jax.ShapeDtypeStruct((4, rows, GROUP), BF16),
        name="gate_norm",
    )(place, y, bc, kept, near, far, first, fade, z_in, *zs, gain, bits)


def per_device(
    x_in, z_in, bc_in, dt_raw, conv_x, conv_bc, a_log, dt_bias, d_skip, gain, sign_bits, out_weight
):
    rows = x_in.shape[0]
    x_here, y_here, t_here = (lax.axis_index(a) for a in ("grp", "sy", "tp"))
    length = lax.axis_size("sz")
    mine = 2 * x_here + y_here
    order = jnp.stack([mine ^ k for k in range(4)]).astype(jnp.int32)
    place = jnp.stack([mine, y_here]).astype(jnp.int32)

    turned = turn(x_here.reshape(1).astype(jnp.int32), out_weight)
    turned = turned.reshape(2, GROUP, out_weight.shape[1])
    across = send(turned, lambda x, z, y, t: (x, z, y, 1 - t))

    x_in, turned = after(x_in, turned)
    packed = pack(order, x_in, bc_in, dt_raw)
    packed, across = after(packed, across)
    own = turned.astype(F32)
    rotated = (across.astype(F32) + jnp.where(t_here == 0, own, -own)).astype(BF16)
    packed, rotated = after(packed, rotated)
    keep = lax.dynamic_index_in_dim(rotated, y_here, 0, keepdims=False)
    given = swap(lax.dynamic_index_in_dim(rotated, 1 - y_here, 0, keepdims=False), 1)
    pieces = [packed[0]] + [swap(packed[k], k) for k in range(1, 4)]
    steps = [packed[4]] + [swap(packed[4 + k], k) for k in range(1, 4)]
    z_in, packed = after(z_in, packed)
    slices = cut(order, z_in)
    given, slices = after(given, slices)
    columns = jnp.where(
        y_here == 0,
        jnp.concatenate([keep, given], axis=1),
        jnp.concatenate([given, keep], axis=1),
    )
    weight = lax.all_gather(columns, "sz", axis=1, tiled=True)
    pieces, columns = after(pieces, columns)
    tails = [p[rows - 16 :] for p in pieces]
    closing = jnp.where(
        y_here == 1, jnp.stack([tails[0], tails[2]]), jnp.stack([tails[1], tails[3]])
    )
    halo = onward(closing, 1)
    slices, pieces = after(slices, pieces)
    zs = [swap(z, k + 1) for k, z in enumerate(slices)]

    xc, bc, low, cum, kept, pair, first, fade = conv_states(
        place, pieces, halo, conv_x, conv_bc, steps, a_log[:, None], dt_bias[:, None]
    )
    near = onward(pair, 1)
    y = within(place, xc, bc, low, cum, jnp.repeat(d_skip, HEADDIM)[None])
    near, (y, zs) = after(near, (y, zs))
    span = join(pair, near)
    distance = 2
    far = onward(span, distance)
    while 2 * distance < length:
        near, span = join(near, far), join(span, far)
        distance *= 2
        far = onward(span, distance)
    act = gate_norm(
        place, y, bc, kept, near, far, first, fade, z_in, zs, gain[None], sign_bits[None]
    )

    half = weight.shape[1] // 2
    theirs = lax.dynamic_slice_in_dim(weight, (1 - t_here) * half, half, 1)
    ours = lax.dynamic_slice_in_dim(weight, t_here * half, half, 1)
    parts = []
    for k in (3, 2, 1, 0):
        away = jnp.dot(act[k], theirs, preferred_element_type=F32).astype(BF16)
        back = send(away, lambda x, z, y, t: (x, z, y, 1 - t))
        stay = jnp.dot(act[k], ours, preferred_element_type=F32) + back.astype(F32)
        parts.append(swap(stay.astype(BF16), k).astype(F32) if k else stay)
    total = parts[3] + parts[2] + parts[1] + parts[0]
    return total.astype(BF16)


def solution(mesh):
    shape = mesh.devices.shape
    fine = Mesh(mesh.devices.reshape(shape[0], shape[1] // 2, 2, shape[2]), AXES)
    seq = ("sz", "sy")
    rows = ("grp",) + seq
    in_specs = (
        P(rows, "tp"),
        P(rows, "tp"),
        P(None, rows, "tp"),
        P(rows, "tp"),
        P(None, "tp"),
        P(None, None, "tp"),
        P("tp"),
        P("tp"),
        P("tp"),
        P("tp"),
        P("tp"),
        P("tp", seq),
    )
    return jax.shard_map(
        per_device, mesh=fine, in_specs=in_specs, out_specs=P(rows, "tp"), check_vma=False
    )
```

```python
import math

import jax
import jax.numpy as jnp
from jax import lax
from jax.experimental import pallas as pl
from jax.experimental.pallas import tpu as pltpu
from jax.sharding import Mesh
from jax.sharding import PartitionSpec as P

HEADDIM = 64
STATE = 128
BLOCK = 256
INNER = 8192
GROUP = 1024
PER = 16
AXES = ("grp", "sz", "sy", "tp")
LOG2E = 1.4426950408889634
F32 = jnp.float32
BF16 = jnp.bfloat16
HIGH = lax.Precision.HIGHEST
VM = pl.BlockSpec(memory_space=pltpu.VMEM)


def send(array, route):
    sizes = [lax.axis_size(a) for a in AXES]
    pairs = []
    for x in range(sizes[0]):
        for z in range(sizes[1]):
            for y in range(sizes[2]):
                for t in range(sizes[3]):
                    to = route(x, z, y, t)
                    if to is None or not 0 <= to[1] < sizes[1]:
                        continue
                    source = ((x * sizes[1] + z) * sizes[2] + y) * sizes[3] + t
                    target = ((to[0] * sizes[1] + to[1]) * sizes[2] + to[2]) * sizes[3] + to[3]
                    pairs.append((source, target))
    return lax.ppermute(array, AXES, pairs)


def swap(array, k):
    return send(array, lambda x, z, y, t: (x ^ (k >> 1), z, y ^ (k & 1), t))


def onward(array, distance):
    return send(array, lambda x, z, y, t: (x, z + distance, y, t))


def after(these, those):
    return lax.optimization_barrier((these, those))


def expander():
    row = lax.broadcasted_iota(jnp.int32, (3 * PER, GROUP), 0)
    lane = lax.broadcasted_iota(jnp.int32, (3 * PER, GROUP), 1)
    return jnp.where(lane // HEADDIM == row % PER, 1.0, 0.0).astype(BF16)


def thirds(v):
    high = v.astype(BF16)
    rest = v - high.astype(F32)
    middle = rest.astype(BF16)
    last = (rest - middle.astype(F32)).astype(BF16)
    return jnp.concatenate([high, middle, last], axis=0)


def widen(terms, spread):
    return lax.dot_general(terms, spread, (((0,), (0,)), ((), ())), preferred_element_type=F32)


def silu(v):
    half = 0.5 * v
    return half + half * jnp.tanh(half)


def pack_kernel(order, x0, x1, x2, x3, b0, b1, b2, b3, dt, o0, o1, o2, o3, d0, d1, d2, d3, e0, e1, e2, e3, turned):
    turned[...] = dt[...].T
    rows = x0.shape[0]
    for k, (x, b, o, d, e) in enumerate(
        ((x0, b0, o0, d0, e0), (x1, b1, o1, d1, e1), (x2, b2, o2, d2, e2), (x3, b3, o3, d3, e3))
    ):
        o[:, :GROUP] = x[...]
        o[:, GROUP : GROUP + STATE] = b[0]
        o[:, GROUP + STATE :] = b[1]
        first = pl.multiple_of(order[k] * PER, PER)
        d[...] = turned[pl.ds(first, PER), :]
        e[...] = o[rows - 16 :, :]


def pack(order, x_in, bc_in, dt_raw):
    rows = x_in.shape[0]
    wide = GROUP + 2 * STATE
    whole = lambda *shape: pl.BlockSpec(shape, lambda i, order: (0,) * len(shape))
    return pl.pallas_call(
        pack_kernel,
        grid_spec=pltpu.PrefetchScalarGridSpec(
            num_scalar_prefetch=1,
            grid=(1,),
            in_specs=[
                pl.BlockSpec((rows, GROUP), lambda i, order, k=k: (0, order[k])) for k in range(4)
            ]
            + [
                pl.BlockSpec((2, rows, STATE), lambda i, order, k=k: (0, 0, order[k]))
                for k in range(4)
            ]
            + [whole(rows, dt_raw.shape[1])],
            out_specs=[whole(rows, wide)] * 4 + [whole(PER, rows)] * 4 + [whole(16, wide)] * 4,
            scratch_shapes=[pltpu.VMEM((dt_raw.shape[1], rows), F32)],
        ),
        out_shape=[jax.ShapeDtypeStruct((rows, wide), BF16)] * 4
        + [jax.ShapeDtypeStruct((PER, rows), F32)] * 4
        + [jax.ShapeDtypeStruct((16, wide), BF16)] * 4,
        name="pack",
    )(order, x_in, x_in, x_in, x_in, bc_in, bc_in, bc_in, bc_in, dt_raw)


def cut_kernel(order, z1, z2, z3, o1, o2, o3):
    o1[...] = z1[...]
    o2[...] = z2[...]
    o3[...] = z3[...]


def cut(order, z_in):
    rows = z_in.shape[0]
    return pl.pallas_call(
        cut_kernel,
        grid_spec=pltpu.PrefetchScalarGridSpec(
            num_scalar_prefetch=1,
            grid=(1,),
            in_specs=[
                pl.BlockSpec((rows, GROUP), lambda i, order, k=k: (0, order[k]))
                for k in range(1, 4)
            ],
            out_specs=[pl.BlockSpec((rows, GROUP), lambda i, order: (0, 0))] * 3,
        ),
        out_shape=[jax.ShapeDtypeStruct((rows, GROUP), BF16)] * 3,
        name="cut",
    )(order, z_in, z_in, z_in)


def turn_kernel(sign, w, out, mid):
    size = 256
    chunks = w.shape[0] // size
    half = chunks // 2
    row = lax.broadcasted_iota(jnp.int32, (size, size), 0)
    col = lax.broadcasted_iota(jnp.int32, (size, size), 1)
    shared = row & col
    parity = jnp.zeros((size, size), jnp.int32)
    for position in range(8):
        parity = parity ^ ((shared >> position) & 1)
    small = (1 - 2 * parity).astype(F32).astype(BF16)
    for j in range(chunks):
        mid[j] = jnp.dot(small, w[j * size : (j + 1) * size, :], preferred_element_type=F32)
    scale = 1.0 / math.sqrt(INNER)
    upper = jnp.where(sign[0] == 0, scale, -scale)

    def step(i, carry):
        at = pl.ds(pl.multiple_of(i * 16, 16), 16)
        values = [mid[j, at, :] * scale + mid[j + half, at, :] * upper for j in range(half)]
        width = 1
        while width < half:
            fresh = list(values)
            for j in range(half):
                if j & width == 0:
                    fresh[j] = values[j] + values[j + width]
                    fresh[j + width] = values[j] - values[j + width]
            values = fresh
            width *= 2
        for j in range(half):
            out[j, at, :] = values[j].astype(BF16)
        return carry

    lax.fori_loop(0, size // 16, step, 0)


def turn(sign, weight):
    rows, cols = weight.shape
    return pl.pallas_call(
        turn_kernel,
        in_specs=[pl.BlockSpec(memory_space=pltpu.SMEM), VM],
        out_specs=VM,
        out_shape=jax.ShapeDtypeStruct((rows // 512, 256, cols), BF16),
        scratch_shapes=[pltpu.VMEM((rows // 256, 256, cols), F32)],
        name="turn",
    )(sign, weight)


def conv_kernel(
    place, p0, p1, p2, p3, halo, cx, cbc, d0, d1, d2, d3, al, db,
    xc, bc, low, cum, kept, pair, first, fade, states, decays,
):
    here = place[1]
    pieces = (p0, p1, p2, p3)
    steps = (d0, d1, d2, d3)
    rows = p0.shape[0]
    spread = expander()
    row = lax.broadcasted_iota(jnp.int32, (rows, rows), 0)
    col = lax.broadcasted_iota(jnp.int32, (rows, rows), 1)
    upto = jnp.where(row <= col, 1.0, 0.0).astype(BF16)
    for k in range(4):
        piece, other = pieces[k], pieces[k ^ 1]
        opening = here == (k & 1)

        def conv(at, taps):
            outer = halo[k >> 1, :, at].astype(F32)
            inner = other[rows - 16 :, at].astype(F32)
            before = jnp.where(opening, outer, inner)[8:]
            padded = jnp.concatenate([before, piece[:, at].astype(F32)], axis=0)
            summed = padded[5 : 5 + rows] * taps[0:1]
            for tap in range(1, 4):
                summed = summed + padded[5 + tap : 5 + tap + rows] * taps[tap : tap + 1]
            return silu(summed).astype(BF16)

        def chunk(c, carry, conv=conv, k=k):
            at = pl.ds(pl.multiple_of(c * 128, 128), 128)
            xc[k, :, at] = conv(at, cx[:, at].astype(F32))
            return carry

        lax.fori_loop(0, GROUP // 128, chunk, 0)
        b = conv(slice(GROUP, GROUP + STATE), cbc[0].astype(F32))
        c = conv(slice(GROUP + STATE, GROUP + 2 * STATE), cbc[1].astype(F32))
        bc[k, :, :STATE] = b
        bc[k, :, STATE:] = c
        raw = steps[k][...] + db[...]
        dt = jnp.maximum(raw, 0.0) + jnp.log1p(jnp.exp(-jnp.abs(raw)))
        rate = -jnp.exp(al[...])
        sums = jnp.dot(thirds(dt * rate), upto, preferred_element_type=F32)
        total = sums[:PER] + sums[PER : 2 * PER] + sums[2 * PER :]
        low[k] = (total - jnp.log(dt)) * LOG2E
        cum[k] = (total * LOG2E).T
        fall = jnp.exp(total)
        kept[k] = thirds(fall)
        wide = widen(thirds(jnp.exp(total[:, rows - 1 :] - total) * dt), spread)
        loaded = (xc[k].astype(F32) * wide).astype(BF16)
        states[k] = lax.dot_general(
            b, loaded, (((0,), (0,)), ((), ())), preferred_element_type=F32
        )
        decays[k] = widen(kept[k, :, rows - 128 :], spread)[120:]
    for r in range(2):
        early, late = 2 * r + here, 2 * r + 1 - here
        decay_early, decay_late = decays[early], decays[late]
        pair[r, :STATE, :] = (states[late] + decay_late[7:8] * states[early]).astype(BF16)
        pair[r, STATE:, :] = split(jnp.broadcast_to((decay_early * decay_late)[7:8], (8, GROUP)))
        first[r] = states[early]
        fade[r] = decay_early


def split(decay):
    high = decay.astype(BF16).astype(F32)
    middle = (decay - high).astype(BF16).astype(F32)
    last = decay - high - middle
    both = jnp.concatenate([decay, decay], axis=0)
    row = lax.broadcasted_iota(jnp.int32, both.shape, 0)
    twice = lambda v: jnp.concatenate([v, v], axis=0)
    out = jnp.where(row == 0, twice(high), jnp.where(row == 1, twice(middle), twice(last)))
    return jnp.where(row < 3, out, 0.0).astype(BF16)


def joined(tail):
    tail = tail.astype(F32)
    return tail[0:1] + tail[1:2] + tail[2:3]


def conv_states(place, pieces, halo, conv_x, conv_bc, steps, a_log, dt_bias):
    rows = pieces[0].shape[0]
    whole = lambda *shape: pl.BlockSpec(shape, lambda i, place: (0,) * len(shape))
    shapes = [
        ((4, rows, GROUP), BF16),
        ((4, rows, 2 * STATE), BF16),
        ((4, PER, rows), F32),
        ((4, rows, PER), F32),
        ((4, 3 * PER, rows), BF16),
        ((2, STATE + 16, GROUP), BF16),
        ((2, STATE, GROUP), F32),
        ((2, 8, GROUP), F32),
    ]
    return pl.pallas_call(
        conv_kernel,
        grid_spec=pltpu.PrefetchScalarGridSpec(
            num_scalar_prefetch=1,
            grid=(1,),
            in_specs=[whole(rows, GROUP + 2 * STATE)] * 4
            + [
                whole(2, 16, GROUP + 2 * STATE),
                pl.BlockSpec((4, GROUP), lambda i, place: (0, place[0])),
                pl.BlockSpec((2, 4, STATE), lambda i, place: (0, 0, place[0])),
            ]
            + [whole(PER, rows)] * 4
            + [pl.BlockSpec((PER, 1), lambda i, place: (place[0], 0))] * 2,
            out_specs=[whole(*shape) for shape, _ in shapes],
            scratch_shapes=[
                pltpu.VMEM((4, STATE, GROUP), F32),
                pltpu.VMEM((4, 8, GROUP), F32),
            ],
        ),
        out_shape=[jax.ShapeDtypeStruct(shape, kind) for shape, kind in shapes],
        name="conv_states",
    )(place, *pieces, halo, conv_x, conv_bc, *steps, a_log, dt_bias)


def join_kernel(late, early, out):
    for r in range(2):
        decay = joined(late[r, STATE:, :])
        out[r, :STATE, :] = (
            late[r, :STATE, :].astype(F32) + decay * early[r, :STATE, :].astype(F32)
        ).astype(BF16)
        both = decay * joined(early[r, STATE:, :])
        out[r, STATE:, :] = split(jnp.broadcast_to(both, (8, GROUP)))


def join(late, early):
    return pl.pallas_call(
        join_kernel,
        in_specs=[VM, VM],
        out_specs=VM,
        out_shape=jax.ShapeDtypeStruct(late.shape, BF16),
        name="join",
    )(late, early)


def within_kernel(place, xc, bc, low, cum, skip, out):
    rows = xc.shape[1]
    half = rows // 2
    b = bc[0, :, :STATE]
    c = bc[0, :, STATE:]
    scores = lax.dot_general(c, b, (((1,), (1,)), ((), ())), preferred_element_type=F32)
    row = lax.broadcasted_iota(jnp.int32, (half, half), 0)
    col = lax.broadcasted_iota(jnp.int32, (half, half), 1)
    causal = row >= col
    corner = jnp.where(causal, scores[:half, :half], 0.0)
    square = scores[half:, :half]
    end = jnp.where(causal, scores[half:, half:], 0.0)
    lane = lax.broadcasted_iota(jnp.int32, (rows, 2 * HEADDIM), 1)
    upright = cum[0]
    for j in range(PER // 2):
        at = slice(j * 2 * HEADDIM, (j + 1) * 2 * HEADDIM)
        x = xc[0, :, at]
        top = bottom = None
        for side in range(2):
            h = 2 * j + side
            mine = jnp.where((lane < HEADDIM) == (side == 0), x, jnp.zeros_like(x))
            level = upright[:, h : h + 1]
            floor = low[0, h : h + 1, :]
            one = jnp.exp2(jnp.minimum(level[:half] - floor[:, :half], 64.0)) * corner
            two = jnp.exp2(level[half:] - floor[:, :half]) * square
            three = jnp.exp2(jnp.minimum(level[half:] - floor[:, half:], 64.0)) * end
            low_rows = jnp.concatenate([two.astype(BF16), three.astype(BF16)], axis=1)
            first = jnp.dot(one.astype(BF16), mine[:half], preferred_element_type=F32)
            last = jnp.dot(low_rows, mine, preferred_element_type=F32)
            top = first if top is None else top + first
            bottom = last if bottom is None else bottom + last
        skipped = x.astype(F32) * skip[:, at]
        out[0, :half, at] = top + skipped[:half]
        out[0, half:, at] = bottom + skipped[half:]


def within(place, xc, bc, low, cum, skip):
    rows = xc.shape[1]
    block = lambda *shape: pl.BlockSpec((1,) + shape, lambda k, place: (k, 0, 0))
    return pl.pallas_call(
        within_kernel,
        grid_spec=pltpu.PrefetchScalarGridSpec(
            num_scalar_prefetch=1,
            grid=(4,),
            in_specs=[
                block(rows, GROUP),
                block(rows, 2 * STATE),
                block(PER, rows),
                block(rows, PER),
                pl.BlockSpec((1, GROUP), lambda k, place: (0, place[0])),
            ],
            out_specs=block(rows, GROUP),
        ),
        out_shape=jax.ShapeDtypeStruct((4, rows, GROUP), F32),
        name="within",
    )(place, xc, bc, low, cum, skip)


def gate_kernel(
    place, y, bc, kept, near, far, first, fade, z0, z1, z2, z3, gain, bits, out, gate
):
    k = pl.program_id(0)
    for index, z in enumerate((z0, z1, z2, z3)):

        @pl.when(k == index)
        def _(z=z):
            gate[...] = silu(z[...].astype(F32))

    opening = place[1] == (k % 2)
    incoming = near[0, :STATE, :].astype(F32) + joined(near[0, STATE:, :]) * far[
        0, :STATE, :
    ].astype(F32)
    incoming = jnp.where(opening, incoming, fade[0, 7:8] * incoming + first[0])
    carried = jnp.dot(bc[0, :, STATE:], incoming.astype(BF16), preferred_element_type=F32)
    gated = (y[0] + widen(kept[0], expander()) * carried) * gate[...]
    scale = lax.rsqrt(jnp.mean(gated * gated, axis=1, keepdims=True) + 1e-05)
    signed = gain[...] * (1 - 2 * bits[...]).astype(F32)
    out[0] = (gated * scale * signed).astype(BF16)


def gate_norm(place, y, bc, kept, near, far, first, fade, z_in, zs, gain, bits):
    rows = y.shape[1]
    block = lambda *shape: pl.BlockSpec((1,) + shape, lambda k, place: (k, 0, 0))
    part = lambda *shape: pl.BlockSpec((1,) + shape, lambda k, place: (k // 2, 0, 0))
    mine = lambda rows: pl.BlockSpec((rows, GROUP), lambda k, place: (0, place[0]))
    return pl.pallas_call(
        gate_kernel,
        grid_spec=pltpu.PrefetchScalarGridSpec(
            num_scalar_prefetch=1,
            grid=(4,),
            in_specs=[
                block(rows, GROUP),
                block(rows, 2 * STATE),
                block(3 * PER, rows),
                part(STATE + 16, GROUP),
                part(STATE + 16, GROUP),
                part(STATE, GROUP),
                part(8, GROUP),
                mine(rows),
            ]
            + [pl.BlockSpec((rows, GROUP), lambda k, place: (0, 0))] * 3
            + [mine(1), mine(1)],
            out_specs=block(rows, GROUP),
            scratch_shapes=[pltpu.VMEM((rows, GROUP), F32)],
        ),
        out_shape=jax.ShapeDtypeStruct((4, rows, GROUP), BF16),
        name="gate_norm",
    )(place, y, bc, kept, near, far, first, fade, z_in, *zs, gain, bits)


def per_device(
    x_in, z_in, bc_in, dt_raw, conv_x, conv_bc, a_log, dt_bias, d_skip, gain, sign_bits, out_weight
):
    rows = x_in.shape[0]
    x_here, y_here, t_here = (lax.axis_index(a) for a in ("grp", "sy", "tp"))
    length = lax.axis_size("sz")
    mine = 2 * x_here + y_here
    order = jnp.stack([mine ^ k for k in range(4)]).astype(jnp.int32)
    place = jnp.stack([mine, y_here]).astype(jnp.int32)

    packed = pack(order, x_in, bc_in, dt_raw)
    out_weight, packed = after(out_weight, packed)
    second = swap(packed[1], 1)
    tails = [
        send(
            packed[8 + k],
            lambda x, z, y, t, k=k: (x ^ (k >> 1), z + 1, y ^ (k & 1), t) if y == 1 else None,
        )
        for k in range(4)
    ]

    turned = turn(x_here.reshape(1).astype(jnp.int32), out_weight)
    turned = turned.reshape(2, GROUP, out_weight.shape[1])
    across = send(turned, lambda x, z, y, t: (x, z, y, 1 - t))
    own = turned.astype(F32)
    rotated = (across.astype(F32) + jnp.where(t_here == 0, own, -own)).astype(BF16)
    rotated, (second, tails) = after(rotated, (second, tails))
    keep = lax.dynamic_index_in_dim(rotated, y_here, 0, keepdims=False)
    given = swap(lax.dynamic_index_in_dim(rotated, 1 - y_here, 0, keepdims=False), 1)
    z_in, packed = after(z_in, packed)
    slices = cut(order, z_in)
    third = swap(packed[2], 2)
    steps = [packed[4]] + [swap(packed[4 + k], k) for k in range(1, 4)]
    given, (slices, third, steps, fourth) = after(given, (slices, third, steps, packed[3]))
    pieces = [packed[0], second, third, swap(fourth, 3)]
    halo = jnp.stack([tails[0] + tails[1], tails[2] + tails[3]])
    columns = jnp.where(
        y_here == 0,
        jnp.concatenate([keep, given], axis=1),
        jnp.concatenate([given, keep], axis=1),
    )
    weight = lax.all_gather(columns, "sz", axis=1, tiled=True)
    pieces, columns = after(pieces, columns)
    slices, pieces = after(slices, pieces)
    zs = [swap(z, k + 1) for k, z in enumerate(slices)]

    xc, bc, low, cum, kept, pair, first, fade = conv_states(
        place, pieces, halo, conv_x, conv_bc, steps, a_log[:, None], dt_bias[:, None]
    )
    near = onward(pair, 1)
    y = within(place, xc, bc, low, cum, jnp.repeat(d_skip, HEADDIM)[None])
    near, (y, zs) = after(near, (y, zs))
    span = join(pair, near)
    distance = 2
    far = onward(span, distance)
    while 2 * distance < length:
        near, span = join(near, far), join(span, far)
        distance *= 2
        far = onward(span, distance)
    act = gate_norm(
        place, y, bc, kept, near, far, first, fade, z_in, zs, gain[None], sign_bits[None]
    )

    half = weight.shape[1] // 2
    theirs = lax.dynamic_slice_in_dim(weight, (1 - t_here) * half, half, 1)
    ours = lax.dynamic_slice_in_dim(weight, t_here * half, half, 1)
    parts = []
    for k in (3, 2, 1, 0):
        away = jnp.dot(act[k], theirs, preferred_element_type=F32).astype(BF16)
        back = send(away, lambda x, z, y, t: (x, z, y, 1 - t))
        stay = jnp.dot(act[k], ours, preferred_element_type=F32) + back.astype(F32)
        parts.append(swap(stay.astype(BF16), k).astype(F32) if k else stay)
    total = parts[3] + parts[2] + parts[1] + parts[0]
    return total.astype(BF16)


def solution(mesh):
    shape = mesh.devices.shape
    fine = Mesh(mesh.devices.reshape(shape[0], shape[1] // 2, 2, shape[2]), AXES)
    seq = ("sz", "sy")
    rows = ("grp",) + seq
    in_specs = (
        P(rows, "tp"),
        P(rows, "tp"),
        P(None, rows, "tp"),
        P(rows, "tp"),
        P(None, "tp"),
        P(None, None, "tp"),
        P("tp"),
        P("tp"),
        P("tp"),
        P("tp"),
        P("tp"),
        P("tp", seq),
    )
    return jax.shard_map(
        per_device, mesh=fine, in_specs=in_specs, out_specs=P(rows, "tp"), check_vma=False
    )
```

```python
import math

import jax
import jax.numpy as jnp
from jax import lax
from jax.experimental import pallas as pl
from jax.experimental.pallas import tpu as pltpu
from jax.sharding import Mesh
from jax.sharding import PartitionSpec as P

HEADDIM = 64
STATE = 128
BLOCK = 256
INNER = 8192
GROUP = 1024
PER = 16
AXES = ("grp", "sz", "sy", "tp")
LOG2E = 1.4426950408889634
F32 = jnp.float32
BF16 = jnp.bfloat16
HIGH = lax.Precision.HIGHEST
VM = pl.BlockSpec(memory_space=pltpu.VMEM)


def send(array, route):
    sizes = [lax.axis_size(a) for a in AXES]
    pairs = []
    for x in range(sizes[0]):
        for z in range(sizes[1]):
            for y in range(sizes[2]):
                for t in range(sizes[3]):
                    to = route(x, z, y, t)
                    if to is None or not 0 <= to[1] < sizes[1]:
                        continue
                    source = ((x * sizes[1] + z) * sizes[2] + y) * sizes[3] + t
                    target = ((to[0] * sizes[1] + to[1]) * sizes[2] + to[2]) * sizes[3] + to[3]
                    pairs.append((source, target))
    return lax.ppermute(array, AXES, pairs)


def swap(array, k):
    return send(array, lambda x, z, y, t: (x ^ (k >> 1), z, y ^ (k & 1), t))


def onward(array, distance):
    return send(array, lambda x, z, y, t: (x, z + distance, y, t))


def after(these, those):
    return lax.optimization_barrier((these, those))


def expander():
    row = lax.broadcasted_iota(jnp.int32, (3 * PER, GROUP), 0)
    lane = lax.broadcasted_iota(jnp.int32, (3 * PER, GROUP), 1)
    return jnp.where(lane // HEADDIM == row % PER, 1.0, 0.0).astype(BF16)


def thirds(v):
    high = v.astype(BF16)
    rest = v - high.astype(F32)
    middle = rest.astype(BF16)
    last = (rest - middle.astype(F32)).astype(BF16)
    return jnp.concatenate([high, middle, last], axis=0)


def widen(terms, spread):
    return lax.dot_general(terms, spread, (((0,), (0,)), ((), ())), preferred_element_type=F32)


def silu(v):
    half = 0.5 * v
    return half + half * jnp.tanh(half)


def pack_kernel(order, x0, x1, x2, x3, b0, b1, b2, b3, dt, o0, o1, o2, o3, d0, d1, d2, d3, e0, e1, e2, e3, turned):
    turned[...] = dt[...].T
    rows = x0.shape[0]
    for k, (x, b, o, d, e) in enumerate(
        ((x0, b0, o0, d0, e0), (x1, b1, o1, d1, e1), (x2, b2, o2, d2, e2), (x3, b3, o3, d3, e3))
    ):
        o[:, :GROUP] = x[...]
        o[:, GROUP : GROUP + STATE] = b[0]
        o[:, GROUP + STATE :] = b[1]
        first = pl.multiple_of(order[k] * PER, PER)
        d[...] = turned[pl.ds(first, PER), :]
        e[...] = o[rows - 16 :, :]


def pack(order, x_in, bc_in, dt_raw):
    rows = x_in.shape[0]
    wide = GROUP + 2 * STATE
    whole = lambda *shape: pl.BlockSpec(shape, lambda i, order: (0,) * len(shape))
    return pl.pallas_call(
        pack_kernel,
        grid_spec=pltpu.PrefetchScalarGridSpec(
            num_scalar_prefetch=1,
            grid=(1,),
            in_specs=[
                pl.BlockSpec((rows, GROUP), lambda i, order, k=k: (0, order[k])) for k in range(4)
            ]
            + [
                pl.BlockSpec((2, rows, STATE), lambda i, order, k=k: (0, 0, order[k]))
                for k in range(4)
            ]
            + [whole(rows, dt_raw.shape[1])],
            out_specs=[whole(rows, wide)] * 4 + [whole(PER, rows)] * 4 + [whole(16, wide)] * 4,
            scratch_shapes=[pltpu.VMEM((dt_raw.shape[1], rows), F32)],
        ),
        out_shape=[jax.ShapeDtypeStruct((rows, wide), BF16)] * 4
        + [jax.ShapeDtypeStruct((PER, rows), F32)] * 4
        + [jax.ShapeDtypeStruct((16, wide), BF16)] * 4,
        name="pack",
    )(order, x_in, x_in, x_in, x_in, bc_in, bc_in, bc_in, bc_in, dt_raw)


def cut_kernel(order, z1, z2, z3, o1, o2, o3):
    o1[...] = z1[...]
    o2[...] = z2[...]
    o3[...] = z3[...]


def cut(order, z_in):
    rows = z_in.shape[0]
    return pl.pallas_call(
        cut_kernel,
        grid_spec=pltpu.PrefetchScalarGridSpec(
            num_scalar_prefetch=1,
            grid=(1,),
            in_specs=[
                pl.BlockSpec((rows, GROUP), lambda i, order, k=k: (0, order[k]))
                for k in range(1, 4)
            ],
            out_specs=[pl.BlockSpec((rows, GROUP), lambda i, order: (0, 0))] * 3,
        ),
        out_shape=[jax.ShapeDtypeStruct((rows, GROUP), BF16)] * 3,
        name="cut",
    )(order, z_in, z_in, z_in)


def turn_kernel(sign, w, out, mid):
    size = 256
    chunks = w.shape[0] // size
    half = chunks // 2
    row = lax.broadcasted_iota(jnp.int32, (size, size), 0)
    col = lax.broadcasted_iota(jnp.int32, (size, size), 1)
    shared = row & col
    parity = jnp.zeros((size, size), jnp.int32)
    for position in range(8):
        parity = parity ^ ((shared >> position) & 1)
    small = (1 - 2 * parity).astype(F32).astype(BF16)
    for j in range(chunks):
        mid[j] = jnp.dot(small, w[j * size : (j + 1) * size, :], preferred_element_type=F32)
    scale = 1.0 / math.sqrt(INNER)
    upper = jnp.where(sign[0] == 0, scale, -scale)

    def step(i, carry):
        at = pl.ds(pl.multiple_of(i * 16, 16), 16)
        values = [mid[j, at, :] * scale + mid[j + half, at, :] * upper for j in range(half)]
        width = 1
        while width < half:
            fresh = list(values)
            for j in range(half):
                if j & width == 0:
                    fresh[j] = values[j] + values[j + width]
                    fresh[j + width] = values[j] - values[j + width]
            values = fresh
            width *= 2
        for j in range(half):
            out[j, at, :] = values[j].astype(BF16)
        return carry

    lax.fori_loop(0, size // 16, step, 0)


def turn(sign, weight):
    rows, cols = weight.shape
    return pl.pallas_call(
        turn_kernel,
        in_specs=[pl.BlockSpec(memory_space=pltpu.SMEM), VM],
        out_specs=VM,
        out_shape=jax.ShapeDtypeStruct((rows // 512, 256, cols), BF16),
        scratch_shapes=[pltpu.VMEM((rows // 256, 256, cols), F32)],
        name="turn",
    )(sign, weight)


def conv_kernel(
    place, p0, p1, p2, p3, halo, cx, cbc, d0, d1, d2, d3, al, db,
    xc, bc, low, cum, kept, pair, first, fade, states, decays,
):
    here = place[1]
    pieces = (p0, p1, p2, p3)
    steps = (d0, d1, d2, d3)
    rows = p0.shape[0]
    spread = expander()
    row = lax.broadcasted_iota(jnp.int32, (rows, rows), 0)
    col = lax.broadcasted_iota(jnp.int32, (rows, rows), 1)
    upto = jnp.where(row <= col, 1.0, 0.0).astype(BF16)
    for k in range(4):
        piece, other = pieces[k], pieces[k ^ 1]
        opening = here == (k & 1)

        def conv(at, taps):
            outer = halo[k >> 1, :, at].astype(F32)
            inner = other[rows - 16 :, at].astype(F32)
            before = jnp.where(opening, outer, inner)[8:]
            padded = jnp.concatenate([before, piece[:, at].astype(F32)], axis=0)
            summed = padded[5 : 5 + rows] * taps[0:1]
            for tap in range(1, 4):
                summed = summed + padded[5 + tap : 5 + tap + rows] * taps[tap : tap + 1]
            return silu(summed).astype(BF16)

        def chunk(c, carry, conv=conv, k=k):
            at = pl.ds(pl.multiple_of(c * 128, 128), 128)
            xc[k, :, at] = conv(at, cx[:, at].astype(F32))
            return carry

        lax.fori_loop(0, GROUP // 128, chunk, 0)
        b = conv(slice(GROUP, GROUP + STATE), cbc[0].astype(F32))
        c = conv(slice(GROUP + STATE, GROUP + 2 * STATE), cbc[1].astype(F32))
        bc[k, :, :STATE] = b
        bc[k, :, STATE:] = c
        raw = steps[k][...] + db[...]
        dt = jnp.maximum(raw, 0.0) + jnp.log1p(jnp.exp(-jnp.abs(raw)))
        rate = -jnp.exp(al[...])
        sums = jnp.dot(thirds(dt * rate), upto, preferred_element_type=F32)
        total = sums[:PER] + sums[PER : 2 * PER] + sums[2 * PER :]
        low[k] = (total - jnp.log(dt)) * LOG2E
        cum[k] = (total * LOG2E).T
        fall = jnp.exp(total)
        kept[k] = thirds(fall)
        wide = widen(thirds(jnp.exp(total[:, rows - 1 :] - total) * dt), spread)
        loaded = (xc[k].astype(F32) * wide).astype(BF16)
        states[k] = lax.dot_general(
            b, loaded, (((0,), (0,)), ((), ())), preferred_element_type=F32
        )
        decays[k] = widen(kept[k, :, rows - 128 :], spread)[120:]
    for r in range(2):
        early, late = 2 * r + here, 2 * r + 1 - here
        decay_early, decay_late = decays[early], decays[late]
        pair[r, :STATE, :] = (states[late] + decay_late[7:8] * states[early]).astype(BF16)
        pair[r, STATE:, :] = split(jnp.broadcast_to((decay_early * decay_late)[7:8], (8, GROUP)))
        first[r] = states[early]
        fade[r] = decay_early


def split(decay):
    high = decay.astype(BF16).astype(F32)
    middle = (decay - high).astype(BF16).astype(F32)
    last = decay - high - middle
    both = jnp.concatenate([decay, decay], axis=0)
    row = lax.broadcasted_iota(jnp.int32, both.shape, 0)
    twice = lambda v: jnp.concatenate([v, v], axis=0)
    out = jnp.where(row == 0, twice(high), jnp.where(row == 1, twice(middle), twice(last)))
    return jnp.where(row < 3, out, 0.0).astype(BF16)


def joined(tail):
    tail = tail.astype(F32)
    return tail[0:1] + tail[1:2] + tail[2:3]


def conv_states(place, pieces, halo, conv_x, conv_bc, steps, a_log, dt_bias):
    rows = pieces[0].shape[0]
    whole = lambda *shape: pl.BlockSpec(shape, lambda i, place: (0,) * len(shape))
    shapes = [
        ((4, rows, GROUP), BF16),
        ((4, rows, 2 * STATE), BF16),
        ((4, PER, rows), F32),
        ((4, rows, PER), F32),
        ((4, 3 * PER, rows), BF16),
        ((2, STATE + 16, GROUP), BF16),
        ((2, STATE, GROUP), F32),
        ((2, 8, GROUP), F32),
    ]
    return pl.pallas_call(
        conv_kernel,
        grid_spec=pltpu.PrefetchScalarGridSpec(
            num_scalar_prefetch=1,
            grid=(1,),
            in_specs=[whole(rows, GROUP + 2 * STATE)] * 4
            + [
                whole(2, 16, GROUP + 2 * STATE),
                pl.BlockSpec((4, GROUP), lambda i, place: (0, place[0])),
                pl.BlockSpec((2, 4, STATE), lambda i, place: (0, 0, place[0])),
            ]
            + [whole(PER, rows)] * 4
            + [pl.BlockSpec((PER, 1), lambda i, place: (place[0], 0))] * 2,
            out_specs=[whole(*shape) for shape, _ in shapes],
            scratch_shapes=[
                pltpu.VMEM((4, STATE, GROUP), F32),
                pltpu.VMEM((4, 8, GROUP), F32),
            ],
        ),
        out_shape=[jax.ShapeDtypeStruct(shape, kind) for shape, kind in shapes],
        name="conv_states",
    )(place, *pieces, halo, conv_x, conv_bc, *steps, a_log, dt_bias)


def join_kernel(late, early, out):
    for r in range(2):
        decay = joined(late[r, STATE:, :])
        out[r, :STATE, :] = (
            late[r, :STATE, :].astype(F32) + decay * early[r, :STATE, :].astype(F32)
        ).astype(BF16)
        both = decay * joined(early[r, STATE:, :])
        out[r, STATE:, :] = split(jnp.broadcast_to(both, (8, GROUP)))


def join(late, early):
    return pl.pallas_call(
        join_kernel,
        in_specs=[VM, VM],
        out_specs=VM,
        out_shape=jax.ShapeDtypeStruct(late.shape, BF16),
        name="join",
    )(late, early)


def within_kernel(place, xc, bc, low, cum, skip, out):
    rows = xc.shape[1]
    half = rows // 2
    b = bc[0, :, :STATE]
    c = bc[0, :, STATE:]
    scores = lax.dot_general(c, b, (((1,), (1,)), ((), ())), preferred_element_type=F32)
    row = lax.broadcasted_iota(jnp.int32, (half, half), 0)
    col = lax.broadcasted_iota(jnp.int32, (half, half), 1)
    causal = row >= col
    corner = jnp.where(causal, scores[:half, :half], 0.0)
    square = scores[half:, :half]
    end = jnp.where(causal, scores[half:, half:], 0.0)
    lane = lax.broadcasted_iota(jnp.int32, (rows, 2 * HEADDIM), 1)
    upright = cum[0]
    for j in range(PER // 2):
        at = slice(j * 2 * HEADDIM, (j + 1) * 2 * HEADDIM)
        x = xc[0, :, at]
        top = bottom = None
        for side in range(2):
            h = 2 * j + side
            mine = jnp.where((lane < HEADDIM) == (side == 0), x, jnp.zeros_like(x))
            level = upright[:, h : h + 1]
            floor = low[0, h : h + 1, :]
            one = jnp.exp2(jnp.minimum(level[:half] - floor[:, :half], 64.0)) * corner
            two = jnp.exp2(level[half:] - floor[:, :half]) * square
            three = jnp.exp2(jnp.minimum(level[half:] - floor[:, half:], 64.0)) * end
            low_rows = jnp.concatenate([two.astype(BF16), three.astype(BF16)], axis=1)
            first = jnp.dot(one.astype(BF16), mine[:half], preferred_element_type=F32)
            last = jnp.dot(low_rows, mine, preferred_element_type=F32)
            top = first if top is None else top + first
            bottom = last if bottom is None else bottom + last
        skipped = x.astype(F32) * skip[:, at]
        out[0, :half, at] = top + skipped[:half]
        out[0, half:, at] = bottom + skipped[half:]


def within(place, xc, bc, low, cum, skip):
    rows = xc.shape[1]
    block = lambda *shape: pl.BlockSpec((1,) + shape, lambda k, place: (k, 0, 0))
    return pl.pallas_call(
        within_kernel,
        grid_spec=pltpu.PrefetchScalarGridSpec(
            num_scalar_prefetch=1,
            grid=(4,),
            in_specs=[
                block(rows, GROUP),
                block(rows, 2 * STATE),
                block(PER, rows),
                block(rows, PER),
                pl.BlockSpec((1, GROUP), lambda k, place: (0, place[0])),
            ],
            out_specs=block(rows, GROUP),
        ),
        out_shape=jax.ShapeDtypeStruct((4, rows, GROUP), F32),
        name="within",
    )(place, xc, bc, low, cum, skip)


def gate_kernel(
    place, y, bc, kept, near, far, first, fade, z0, z1, z2, z3, gain, bits, out, gate
):
    k = pl.program_id(0)
    for index, z in enumerate((z0, z1, z2, z3)):

        @pl.when(k == index)
        def _(z=z):
            gate[...] = silu(z[...].astype(F32))

    opening = place[1] == (k % 2)
    incoming = near[0, :STATE, :].astype(F32) + joined(near[0, STATE:, :]) * far[
        0, :STATE, :
    ].astype(F32)
    incoming = jnp.where(opening, incoming, fade[0, 7:8] * incoming + first[0])
    carried = jnp.dot(bc[0, :, STATE:], incoming.astype(BF16), preferred_element_type=F32)
    gated = (y[0] + widen(kept[0], expander()) * carried) * gate[...]
    scale = lax.rsqrt(jnp.mean(gated * gated, axis=1, keepdims=True) + 1e-05)
    signed = gain[...] * (1 - 2 * bits[...]).astype(F32)
    out[0] = (gated * scale * signed).astype(BF16)


def gate_norm(place, y, bc, kept, near, far, first, fade, z_in, zs, gain, bits):
    rows = y.shape[1]
    block = lambda *shape: pl.BlockSpec((1,) + shape, lambda k, place: (k, 0, 0))
    part = lambda *shape: pl.BlockSpec((1,) + shape, lambda k, place: (k // 2, 0, 0))
    mine = lambda rows: pl.BlockSpec((rows, GROUP), lambda k, place: (0, place[0]))
    return pl.pallas_call(
        gate_kernel,
        grid_spec=pltpu.PrefetchScalarGridSpec(
            num_scalar_prefetch=1,
            grid=(4,),
            in_specs=[
                block(rows, GROUP),
                block(rows, 2 * STATE),
                block(3 * PER, rows),
                part(STATE + 16, GROUP),
                part(STATE + 16, GROUP),
                part(STATE, GROUP),
                part(8, GROUP),
                mine(rows),
            ]
            + [pl.BlockSpec((rows, GROUP), lambda k, place: (0, 0))] * 3
            + [mine(1), mine(1)],
            out_specs=block(rows, GROUP),
            scratch_shapes=[pltpu.VMEM((rows, GROUP), F32)],
        ),
        out_shape=jax.ShapeDtypeStruct((4, rows, GROUP), BF16),
        name="gate_norm",
    )(place, y, bc, kept, near, far, first, fade, z_in, *zs, gain, bits)


def per_device(
    x_in, z_in, bc_in, dt_raw, conv_x, conv_bc, a_log, dt_bias, d_skip, gain, sign_bits, out_weight
):
    rows = x_in.shape[0]
    x_here, y_here, t_here = (lax.axis_index(a) for a in ("grp", "sy", "tp"))
    length = lax.axis_size("sz")
    mine = 2 * x_here + y_here
    order = jnp.stack([mine ^ k for k in range(4)]).astype(jnp.int32)
    place = jnp.stack([mine, y_here]).astype(jnp.int32)

    turned = turn(x_here.reshape(1).astype(jnp.int32), out_weight)
    turned = turned.reshape(2, GROUP, out_weight.shape[1])
    across = send(turned, lambda x, z, y, t: (x, z, y, 1 - t))

    x_in, turned = after(x_in, turned)
    packed = pack(order, x_in, bc_in, dt_raw)
    packed, across = after(packed, across)
    own = turned.astype(F32)
    rotated = (across.astype(F32) + jnp.where(t_here == 0, own, -own)).astype(BF16)
    packed, rotated = after(packed, rotated)
    keep = lax.dynamic_index_in_dim(rotated, y_here, 0, keepdims=False)
    given = swap(lax.dynamic_index_in_dim(rotated, 1 - y_here, 0, keepdims=False), 1)
    pieces = [packed[0]] + [swap(packed[k], k) for k in range(1, 4)]
    steps = [packed[4]] + [swap(packed[4 + k], k) for k in range(1, 4)]
    z_in, packed = after(z_in, packed)
    slices = cut(order, z_in)
    tails = [
        send(
            packed[8 + k],
            lambda x, z, y, t, k=k: (x ^ (k >> 1), z + 1, y ^ (k & 1), t) if y == 1 else None,
        )
        for k in range(4)
    ]
    given, (slices, tails) = after(given, (slices, tails))
    halo = jnp.stack([tails[0] + tails[1], tails[2] + tails[3]])
    columns = jnp.where(
        y_here == 0,
        jnp.concatenate([keep, given], axis=1),
        jnp.concatenate([given, keep], axis=1),
    )
    weight = lax.all_gather(columns, "sz", axis=1, tiled=True)
    pieces, columns = after(pieces, columns)
    slices, pieces = after(slices, pieces)
    zs = [swap(z, k + 1) for k, z in enumerate(slices)]

    xc, bc, low, cum, kept, pair, first, fade = conv_states(
        place, pieces, halo, conv_x, conv_bc, steps, a_log[:, None], dt_bias[:, None]
    )
    near = onward(pair, 1)
    y = within(place, xc, bc, low, cum, jnp.repeat(d_skip, HEADDIM)[None])
    near, (y, zs) = after(near, (y, zs))
    span = join(pair, near)
    distance = 2
    far = onward(span, distance)
    while 2 * distance < length:
        near, span = join(near, far), join(span, far)
        distance *= 2
        far = onward(span, distance)
    act = gate_norm(
        place, y, bc, kept, near, far, first, fade, z_in, zs, gain[None], sign_bits[None]
    )

    half = weight.shape[1] // 2
    theirs = lax.dynamic_slice_in_dim(weight, (1 - t_here) * half, half, 1)
    ours = lax.dynamic_slice_in_dim(weight, t_here * half, half, 1)
    parts = []
    for k in (3, 2, 1, 0):
        away = jnp.dot(act[k], theirs, preferred_element_type=F32).astype(BF16)
        back = send(away, lambda x, z, y, t: (x, z, y, 1 - t))
        stay = jnp.dot(act[k], ours, preferred_element_type=F32) + back.astype(F32)
        parts.append(swap(stay.astype(BF16), k).astype(F32) if k else stay)
    total = parts[3] + parts[2] + parts[1] + parts[0]
    return total.astype(BF16)


def solution(mesh):
    shape = mesh.devices.shape
    fine = Mesh(mesh.devices.reshape(shape[0], shape[1] // 2, 2, shape[2]), AXES)
    seq = ("sz", "sy")
    rows = ("grp",) + seq
    in_specs = (
        P(rows, "tp"),
        P(rows, "tp"),
        P(None, rows, "tp"),
        P(rows, "tp"),
        P(None, "tp"),
        P(None, None, "tp"),
        P("tp"),
        P("tp"),
        P("tp"),
        P("tp"),
        P("tp"),
        P("tp", seq),
    )
    return jax.shard_map(
        per_device, mesh=fine, in_specs=in_specs, out_specs=P(rows, "tp"), check_vma=False
    )
```

```python
import functools
import math

import jax
import jax.numpy as jnp
from jax import lax
from jax.experimental import pallas as pl
from jax.experimental.pallas import tpu as pltpu
from jax.sharding import Mesh
from jax.sharding import PartitionSpec as P

HEADDIM = 64
STATE = 128
BLOCK = 256
INNER = 8192
GROUP = 1024
PER = 16
AXES = ("grp", "sz", "sy", "tp")
LOG2E = 1.4426950408889634
F32 = jnp.float32
BF16 = jnp.bfloat16
HIGH = lax.Precision.HIGHEST
VM = pl.BlockSpec(memory_space=pltpu.VMEM)


def send(array, route):
    sizes = [lax.axis_size(a) for a in AXES]
    pairs = []
    for x in range(sizes[0]):
        for z in range(sizes[1]):
            for y in range(sizes[2]):
                for t in range(sizes[3]):
                    to = route(x, z, y, t)
                    if to is None or not 0 <= to[1] < sizes[1]:
                        continue
                    source = ((x * sizes[1] + z) * sizes[2] + y) * sizes[3] + t
                    target = ((to[0] * sizes[1] + to[1]) * sizes[2] + to[2]) * sizes[3] + to[3]
                    pairs.append((source, target))
    return lax.ppermute(array, AXES, pairs)


def swap(array, k):
    return send(array, lambda x, z, y, t: (x ^ (k >> 1), z, y ^ (k & 1), t))


def onward(array, distance):
    return send(array, lambda x, z, y, t: (x, z + distance, y, t))


def after(these, those):
    return lax.optimization_barrier((these, those))


def expander():
    row = lax.broadcasted_iota(jnp.int32, (3 * PER, GROUP), 0)
    lane = lax.broadcasted_iota(jnp.int32, (3 * PER, GROUP), 1)
    return jnp.where(lane // HEADDIM == row % PER, 1.0, 0.0).astype(BF16)


def thirds(v):
    high = v.astype(BF16)
    rest = v - high.astype(F32)
    middle = rest.astype(BF16)
    last = (rest - middle.astype(F32)).astype(BF16)
    return jnp.concatenate([high, middle, last], axis=0)


def widen(terms, spread):
    return lax.dot_general(terms, spread, (((0,), (0,)), ((), ())), preferred_element_type=F32)


def silu(v):
    half = 0.5 * v
    return half + half * jnp.tanh(half)


def pack_kernel(order, x0, x1, x2, x3, b0, b1, b2, b3, dt, o0, o1, o2, o3, d0, d1, d2, d3, e0, e1, e2, e3, turned):
    turned[...] = dt[...].T
    rows = x0.shape[0]
    for k, (x, b, o, d, e) in enumerate(
        ((x0, b0, o0, d0, e0), (x1, b1, o1, d1, e1), (x2, b2, o2, d2, e2), (x3, b3, o3, d3, e3))
    ):
        o[:, :GROUP] = x[...]
        o[:, GROUP : GROUP + STATE] = b[0]
        o[:, GROUP + STATE :] = b[1]
        first = pl.multiple_of(order[k] * PER, PER)
        d[...] = turned[pl.ds(first, PER), :]
        e[...] = o[rows - 16 :, :]


def pack(order, x_in, bc_in, dt_raw):
    rows = x_in.shape[0]
    wide = GROUP + 2 * STATE
    whole = lambda *shape: pl.BlockSpec(shape, lambda i, order: (0,) * len(shape))
    return pl.pallas_call(
        pack_kernel,
        grid_spec=pltpu.PrefetchScalarGridSpec(
            num_scalar_prefetch=1,
            grid=(1,),
            in_specs=[
                pl.BlockSpec((rows, GROUP), lambda i, order, k=k: (0, order[k])) for k in range(4)
            ]
            + [
                pl.BlockSpec((2, rows, STATE), lambda i, order, k=k: (0, 0, order[k]))
                for k in range(4)
            ]
            + [whole(rows, dt_raw.shape[1])],
            out_specs=[whole(rows, wide)] * 4 + [whole(PER, rows)] * 4 + [whole(16, wide)] * 4,
            scratch_shapes=[pltpu.VMEM((dt_raw.shape[1], rows), F32)],
        ),
        out_shape=[jax.ShapeDtypeStruct((rows, wide), BF16)] * 4
        + [jax.ShapeDtypeStruct((PER, rows), F32)] * 4
        + [jax.ShapeDtypeStruct((16, wide), BF16)] * 4,
        name="pack",
    )(order, x_in, x_in, x_in, x_in, bc_in, bc_in, bc_in, bc_in, dt_raw)


def cut_kernel(order, z1, z2, z3, o1, o2, o3):
    o1[...] = z1[...]
    o2[...] = z2[...]
    o3[...] = z3[...]


def cut(order, z_in):
    rows = z_in.shape[0]
    return pl.pallas_call(
        cut_kernel,
        grid_spec=pltpu.PrefetchScalarGridSpec(
            num_scalar_prefetch=1,
            grid=(1,),
            in_specs=[
                pl.BlockSpec((rows, GROUP), lambda i, order, k=k: (0, order[k]))
                for k in range(1, 4)
            ],
            out_specs=[pl.BlockSpec((rows, GROUP), lambda i, order: (0, 0))] * 3,
        ),
        out_shape=[jax.ShapeDtypeStruct((rows, GROUP), BF16)] * 3,
        name="cut",
    )(order, z_in, z_in, z_in)


def turn_kernel(sign, w, out, mid):
    size = 256
    chunks = w.shape[0] // size
    half = chunks // 2
    row = lax.broadcasted_iota(jnp.int32, (size, size), 0)
    col = lax.broadcasted_iota(jnp.int32, (size, size), 1)
    shared = row & col
    parity = jnp.zeros((size, size), jnp.int32)
    for position in range(8):
        parity = parity ^ ((shared >> position) & 1)
    small = (1 - 2 * parity).astype(F32).astype(BF16)
    for j in range(chunks):
        mid[j] = jnp.dot(small, w[j * size : (j + 1) * size, :], preferred_element_type=F32)
    scale = 1.0 / math.sqrt(INNER)
    upper = jnp.where(sign[0] == 0, scale, -scale)

    def step(i, carry):
        at = pl.ds(pl.multiple_of(i * 16, 16), 16)
        values = [mid[j, at, :] * scale + mid[j + half, at, :] * upper for j in range(half)]
        width = 1
        while width < half:
            fresh = list(values)
            for j in range(half):
                if j & width == 0:
                    fresh[j] = values[j] + values[j + width]
                    fresh[j + width] = values[j] - values[j + width]
            values = fresh
            width *= 2
        for j in range(half):
            out[j, at, :] = values[j].astype(BF16)
        return carry

    lax.fori_loop(0, size // 16, step, 0)


def turn(sign, weight):
    rows, cols = weight.shape
    return pl.pallas_call(
        turn_kernel,
        in_specs=[pl.BlockSpec(memory_space=pltpu.SMEM), VM],
        out_specs=VM,
        out_shape=jax.ShapeDtypeStruct((rows // 512, 256, cols), BF16),
        scratch_shapes=[pltpu.VMEM((rows // 256, 256, cols), F32)],
        name="turn",
    )(sign, weight)


def conv_kernel(
    place, p0, p1, p2, p3, halo, cx, cbc, d0, d1, d2, d3, al, db,
    xc, bc, low, cum, kept, pair, first, fade, states, decays,
):
    here = place[1]
    pieces = (p0, p1, p2, p3)
    steps = (d0, d1, d2, d3)
    rows = p0.shape[0]
    spread = expander()
    row = lax.broadcasted_iota(jnp.int32, (rows, rows), 0)
    col = lax.broadcasted_iota(jnp.int32, (rows, rows), 1)
    upto = jnp.where(row <= col, 1.0, 0.0).astype(BF16)
    for k in range(4):
        piece, other = pieces[k], pieces[k ^ 1]
        opening = here == (k & 1)

        def conv(at, taps):
            outer = halo[k >> 1, :, at].astype(F32)
            inner = other[rows - 16 :, at].astype(F32)
            before = jnp.where(opening, outer, inner)[8:]
            padded = jnp.concatenate([before, piece[:, at].astype(F32)], axis=0)
            summed = padded[5 : 5 + rows] * taps[0:1]
            for tap in range(1, 4):
                summed = summed + padded[5 + tap : 5 + tap + rows] * taps[tap : tap + 1]
            return silu(summed).astype(BF16)

        def chunk(c, carry, conv=conv, k=k):
            at = pl.ds(pl.multiple_of(c * 128, 128), 128)
            xc[k, :, at] = conv(at, cx[:, at].astype(F32))
            return carry

        lax.fori_loop(0, GROUP // 128, chunk, 0)
        b = conv(slice(GROUP, GROUP + STATE), cbc[0].astype(F32))
        c = conv(slice(GROUP + STATE, GROUP + 2 * STATE), cbc[1].astype(F32))
        bc[k, :, :STATE] = b
        bc[k, :, STATE:] = c
        raw = steps[k][...] + db[...]
        dt = jnp.maximum(raw, 0.0) + jnp.log1p(jnp.exp(-jnp.abs(raw)))
        rate = -jnp.exp(al[...])
        sums = jnp.dot(thirds(dt * rate), upto, preferred_element_type=F32)
        total = sums[:PER] + sums[PER : 2 * PER] + sums[2 * PER :]
        low[k] = (total - jnp.log(dt)) * LOG2E
        cum[k] = (total * LOG2E).T
        fall = jnp.exp(total)
        kept[k] = thirds(fall)
        wide = widen(thirds(jnp.exp(total[:, rows - 1 :] - total) * dt), spread)
        loaded = (xc[k].astype(F32) * wide).astype(BF16)
        states[k] = lax.dot_general(
            b, loaded, (((0,), (0,)), ((), ())), preferred_element_type=F32
        )
        decays[k] = widen(kept[k, :, rows - 128 :], spread)[120:]
    for r in range(2):
        early, late = 2 * r + here, 2 * r + 1 - here
        decay_early, decay_late = decays[early], decays[late]
        pair[r, :STATE, :] = (states[late] + decay_late[7:8] * states[early]).astype(BF16)
        pair[r, STATE:, :] = split(jnp.broadcast_to((decay_early * decay_late)[7:8], (8, GROUP)))
        first[r] = states[early]
        fade[r] = decay_early


def split(decay):
    high = decay.astype(BF16).astype(F32)
    middle = (decay - high).astype(BF16).astype(F32)
    last = decay - high - middle
    both = jnp.concatenate([decay, decay], axis=0)
    row = lax.broadcasted_iota(jnp.int32, both.shape, 0)
    twice = lambda v: jnp.concatenate([v, v], axis=0)
    out = jnp.where(row == 0, twice(high), jnp.where(row == 1, twice(middle), twice(last)))
    return jnp.where(row < 3, out, 0.0).astype(BF16)


def joined(tail):
    tail = tail.astype(F32)
    return tail[0:1] + tail[1:2] + tail[2:3]


def conv_states(place, pieces, halo, conv_x, conv_bc, steps, a_log, dt_bias):
    rows = pieces[0].shape[0]
    whole = lambda *shape: pl.BlockSpec(shape, lambda i, place: (0,) * len(shape))
    shapes = [
        ((4, rows, GROUP), BF16),
        ((4, rows, 2 * STATE), BF16),
        ((4, PER, rows), F32),
        ((4, rows, PER), F32),
        ((4, 3 * PER, rows), BF16),
        ((2, STATE + 16, GROUP), BF16),
        ((2, STATE, GROUP), F32),
        ((2, 8, GROUP), F32),
    ]
    return pl.pallas_call(
        conv_kernel,
        grid_spec=pltpu.PrefetchScalarGridSpec(
            num_scalar_prefetch=1,
            grid=(1,),
            in_specs=[whole(rows, GROUP + 2 * STATE)] * 4
            + [
                whole(2, 16, GROUP + 2 * STATE),
                pl.BlockSpec((4, GROUP), lambda i, place: (0, place[0])),
                pl.BlockSpec((2, 4, STATE), lambda i, place: (0, 0, place[0])),
            ]
            + [whole(PER, rows)] * 4
            + [pl.BlockSpec((PER, 1), lambda i, place: (place[0], 0))] * 2,
            out_specs=[whole(*shape) for shape, _ in shapes],
            scratch_shapes=[
                pltpu.VMEM((4, STATE, GROUP), F32),
                pltpu.VMEM((4, 8, GROUP), F32),
            ],
        ),
        out_shape=[jax.ShapeDtypeStruct(shape, kind) for shape, kind in shapes],
        name="conv_states",
    )(place, *pieces, halo, conv_x, conv_bc, *steps, a_log, dt_bias)


def join_kernel(late, early, out):
    for r in range(2):
        decay = joined(late[r, STATE:, :])
        out[r, :STATE, :] = (
            late[r, :STATE, :].astype(F32) + decay * early[r, :STATE, :].astype(F32)
        ).astype(BF16)
        both = decay * joined(early[r, STATE:, :])
        out[r, STATE:, :] = split(jnp.broadcast_to(both, (8, GROUP)))


def join(late, early):
    return pl.pallas_call(
        join_kernel,
        in_specs=[VM, VM],
        out_specs=VM,
        out_shape=jax.ShapeDtypeStruct(late.shape, BF16),
        name="join",
    )(late, early)


def within_kernel(place, xc, bc, low, cum, skip, out):
    rows = xc.shape[1]
    half = rows // 2
    b = bc[0, :, :STATE]
    c = bc[0, :, STATE:]
    scores = lax.dot_general(c, b, (((1,), (1,)), ((), ())), preferred_element_type=F32)
    row = lax.broadcasted_iota(jnp.int32, (half, half), 0)
    col = lax.broadcasted_iota(jnp.int32, (half, half), 1)
    causal = row >= col
    corner = jnp.where(causal, scores[:half, :half], 0.0)
    square = scores[half:, :half]
    end = jnp.where(causal, scores[half:, half:], 0.0)
    lane = lax.broadcasted_iota(jnp.int32, (rows, 2 * HEADDIM), 1)
    upright = cum[0]
    for j in range(PER // 2):
        at = slice(j * 2 * HEADDIM, (j + 1) * 2 * HEADDIM)
        x = xc[0, :, at]
        top = bottom = None
        for side in range(2):
            h = 2 * j + side
            mine = jnp.where((lane < HEADDIM) == (side == 0), x, jnp.zeros_like(x))
            level = upright[:, h : h + 1]
            floor = low[0, h : h + 1, :]
            one = jnp.exp2(jnp.minimum(level[:half] - floor[:, :half], 64.0)) * corner
            two = jnp.exp2(level[half:] - floor[:, :half]) * square
            three = jnp.exp2(jnp.minimum(level[half:] - floor[:, half:], 64.0)) * end
            low_rows = jnp.concatenate([two.astype(BF16), three.astype(BF16)], axis=1)
            first = jnp.dot(one.astype(BF16), mine[:half], preferred_element_type=F32)
            last = jnp.dot(low_rows, mine, preferred_element_type=F32)
            top = first if top is None else top + first
            bottom = last if bottom is None else bottom + last
        skipped = x.astype(F32) * skip[:, at]
        out[0, :half, at] = top + skipped[:half]
        out[0, half:, at] = bottom + skipped[half:]


def within(place, xc, bc, low, cum, skip):
    rows = xc.shape[1]
    block = lambda *shape: pl.BlockSpec((1,) + shape, lambda k, place: (k, 0, 0))
    return pl.pallas_call(
        within_kernel,
        grid_spec=pltpu.PrefetchScalarGridSpec(
            num_scalar_prefetch=1,
            grid=(4,),
            in_specs=[
                block(rows, GROUP),
                block(rows, 2 * STATE),
                block(PER, rows),
                block(rows, PER),
                pl.BlockSpec((1, GROUP), lambda k, place: (0, place[0])),
            ],
            out_specs=block(rows, GROUP),
        ),
        out_shape=jax.ShapeDtypeStruct((4, rows, GROUP), F32),
        name="within",
    )(place, xc, bc, low, cum, skip)


def gate_kernel(k, place, y, bc, kept, near, far, first, fade, z, gain, bits, out):
    opening = place[1] == (k % 2)
    incoming = near[0, :STATE, :].astype(F32) + joined(near[0, STATE:, :]) * far[
        0, :STATE, :
    ].astype(F32)
    incoming = jnp.where(opening, incoming, fade[0, 7:8] * incoming + first[0])
    carried = jnp.dot(bc[0, :, STATE:], incoming.astype(BF16), preferred_element_type=F32)
    gated = (y[0] + widen(kept[0], expander()) * carried) * silu(z[...].astype(F32))
    scale = lax.rsqrt(jnp.mean(gated * gated, axis=1, keepdims=True) + 1e-05)
    signed = gain[...] * (1 - 2 * bits[...]).astype(F32)
    out[...] = (gated * scale * signed).astype(BF16)


def gate_norm(k, place, y, bc, kept, near, far, first, fade, z, gain, bits):
    rows = y.shape[1]
    block = lambda *shape: pl.BlockSpec((1,) + shape, lambda i, place: (k, 0, 0))
    part = lambda *shape: pl.BlockSpec((1,) + shape, lambda i, place: (k // 2, 0, 0))
    mine = lambda rows: pl.BlockSpec((rows, GROUP), lambda i, place: (0, place[0]))
    whole = pl.BlockSpec((rows, GROUP), lambda i, place: (0, 0))
    return pl.pallas_call(
        functools.partial(gate_kernel, k),
        grid_spec=pltpu.PrefetchScalarGridSpec(
            num_scalar_prefetch=1,
            grid=(1,),
            in_specs=[
                block(rows, GROUP),
                block(rows, 2 * STATE),
                block(3 * PER, rows),
                part(STATE + 16, GROUP),
                part(STATE + 16, GROUP),
                part(STATE, GROUP),
                part(8, GROUP),
                whole if k else mine(rows),
                mine(1),
                mine(1),
            ],
            out_specs=whole,
        ),
        out_shape=jax.ShapeDtypeStruct((rows, GROUP), BF16),
        name="gate_norm",
    )(place, y, bc, kept, near, far, first, fade, z, gain, bits)


def per_device(
    x_in, z_in, bc_in, dt_raw, conv_x, conv_bc, a_log, dt_bias, d_skip, gain, sign_bits, out_weight
):
    rows = x_in.shape[0]
    x_here, y_here, t_here = (lax.axis_index(a) for a in ("grp", "sy", "tp"))
    length = lax.axis_size("sz")
    mine = 2 * x_here + y_here
    order = jnp.stack([mine ^ k for k in range(4)]).astype(jnp.int32)
    place = jnp.stack([mine, y_here]).astype(jnp.int32)

    turned = turn(x_here.reshape(1).astype(jnp.int32), out_weight)
    turned = turned.reshape(2, GROUP, out_weight.shape[1])
    across = send(turned, lambda x, z, y, t: (x, z, y, 1 - t))

    x_in, turned = after(x_in, turned)
    packed = pack(order, x_in, bc_in, dt_raw)
    packed, across = after(packed, across)
    own = turned.astype(F32)
    rotated = (across.astype(F32) + jnp.where(t_here == 0, own, -own)).astype(BF16)
    packed, rotated = after(packed, rotated)
    keep = lax.dynamic_index_in_dim(rotated, y_here, 0, keepdims=False)
    given = swap(lax.dynamic_index_in_dim(rotated, 1 - y_here, 0, keepdims=False), 1)
    pieces = [packed[0]] + [swap(packed[k], k) for k in range(1, 4)]
    steps = [packed[4]] + [swap(packed[4 + k], k) for k in range(1, 4)]
    z_in, packed = after(z_in, packed)
    slices = cut(order, z_in)
    tails = [
        send(
            packed[8 + k],
            lambda x, z, y, t, k=k: (x ^ (k >> 1), z + 1, y ^ (k & 1), t) if y == 1 else None,
        )
        for k in range(4)
    ]
    given, (slices, tails) = after(given, (slices, tails))
    halo = jnp.stack([tails[0] + tails[1], tails[2] + tails[3]])
    columns = jnp.where(
        y_here == 0,
        jnp.concatenate([keep, given], axis=1),
        jnp.concatenate([given, keep], axis=1),
    )
    weight = lax.all_gather(columns, "sz", axis=1, tiled=True)
    pieces, columns = after(pieces, columns)
    slices, pieces = after(slices, pieces)
    zs = [swap(z, k + 1) for k, z in enumerate(slices)]

    xc, bc, low, cum, kept, pair, first, fade = conv_states(
        place, pieces, halo, conv_x, conv_bc, steps, a_log[:, None], dt_bias[:, None]
    )
    near = onward(pair, 1)
    y = within(place, xc, bc, low, cum, jnp.repeat(d_skip, HEADDIM)[None])
    near, (y, zs) = after(near, (y, zs))
    span = join(pair, near)
    distance = 2
    far = onward(span, distance)
    while 2 * distance < length:
        near, span = join(near, far), join(span, far)
        distance *= 2
        far = onward(span, distance)
    gates = [z_in] + zs

    half = weight.shape[1] // 2
    theirs = lax.dynamic_slice_in_dim(weight, (1 - t_here) * half, half, 1)
    ours = lax.dynamic_slice_in_dim(weight, t_here * half, half, 1)
    parts = []
    for k in (3, 2, 1, 0):
        act = gate_norm(
            k, place, y, bc, kept, near, far, first, fade, gates[k], gain[None], sign_bits[None]
        )
        away = jnp.dot(act, theirs, preferred_element_type=F32).astype(BF16)
        back = send(away, lambda x, z, y, t: (x, z, y, 1 - t))
        stay = jnp.dot(act, ours, preferred_element_type=F32) + back.astype(F32)
        far, stay = after(far, stay)
        parts.append(swap(stay.astype(BF16), k).astype(F32) if k else stay)
    total = parts[3] + parts[2] + parts[1] + parts[0]
    return total.astype(BF16)


def solution(mesh):
    shape = mesh.devices.shape
    fine = Mesh(mesh.devices.reshape(shape[0], shape[1] // 2, 2, shape[2]), AXES)
    seq = ("sz", "sy")
    rows = ("grp",) + seq
    in_specs = (
        P(rows, "tp"),
        P(rows, "tp"),
        P(None, rows, "tp"),
        P(rows, "tp"),
        P(None, "tp"),
        P(None, None, "tp"),
        P("tp"),
        P("tp"),
        P("tp"),
        P("tp"),
        P("tp"),
        P("tp", seq),
    )
    return jax.shard_map(
        per_device, mesh=fine, in_specs=in_specs, out_specs=P(rows, "tp"), check_vma=False
    )
```
